128 devices in a mesh: dp: 4 (over x), db: 32 (over z, y, core).
Axes of the slice: x: 4, y: 4, z: 4, core: 2. Of those that a mesh axis runs over, the one named last changes fastest.
Arguments:
- tokens: bfloat16 [2048, 64, 1024], P(('dp', 'db')), may hold values from -6 to 6
- neighbours: int32 [2048, 2], P(('dp', 'db')), may hold values from 0 to 2047, as said below
- database: bfloat16 [2048, 64, 1024], P('db'), may hold values from -256 to 256
- norm_gain: float32 [1024], replicated, may hold values from 0.1 to 1.9
- q_weight: bfloat16 [1024, 1024], P(('dp', 'db')), may hold values from -0.1875 to 0.1875
- key_weight: bfloat16 [1024, 1024], P(('dp', 'db')), may hold values from -0.1875 to 0.1875
- value_weight: bfloat16 [1024, 1024], P(('dp', 'db')), may hold values from -0.1875 to 0.1875
- out_weight: bfloat16 [1024, 1024], P(('dp', 'db')), may hold values from -0.1875 to 0.1875
Outputs:
- mixed: bfloat16 [2048, 64, 1024], P(('dp', 'db'))
The draws below stay inside these ranges and needn't reach their ends.
Inputs may be any that keep to these rules, and one draw needn't show every extreme that they name: The two neighbours of a span are different database spans. Among the 32 neighbours of the spans of one device, at most 2 lie in one index of db's 64 spans; in every draw, for each index of dp, some index of db receives exactly 2 from every device of that dp index.
All inputs are finite; a program needn't handle non-finite values.
Results may differ from the reference program's by a relative error of at most 0.0035.
The reference program's roundings to bfloat16 on the way (of `normed`, `queries`, `fetched`, `probs` and `attended`) count: a program that leaves them out, or rounds other values in their place, can miss the bound.
Values may be sent and summed in bfloat16 or wider, within the bound.
No kernel may reach another device: no remote copies, remote signals or barrier semaphores. Data moves between devices by JAX's collectives and lax.ppermute only.
A program may use at most 128 MiB of HBM per device.

```python
import math
import jax
import jax.numpy as jnp
from jax import lax

D = 1024
HEADS = 16
LEN = 64
NEIGH = 2
CH_DEV = 16
DB_DEV = 64
SPANS = 2048
DB_SPANS = 2048
CAP = 2


def draw_neighbours(key, part):
    devices = SPANS // CH_DEV
    holders = DB_SPANS // DB_DEV
    dp_count = devices // holders
    needed = 2 * CH_DEV
    copies_n = holders * CAP
    keys = jax.random.split(jax.random.fold_in(key, 7), 5)
    hot_row = jax.random.randint(keys[0], (dp_count,), 0, holders)
    hot = jnp.repeat(hot_row, holders)
    copies = jnp.tile(jnp.arange(holders, dtype=jnp.int32), CAP)
    spots = jnp.arange(copies_n, dtype=jnp.int32)
    scores = jax.random.randint(keys[1], (devices, copies_n), 0, 1 << 20) * copies_n + spots[None, :]
    scores = jnp.where(copies[None, :] == hot[:, None], spots[None, :] - copies_n, scores)
    order = jnp.argsort(scores, axis=1)[:, :needed]
    picked = copies[order]
    mixing = jax.random.randint(keys[2], (devices, needed), 0, 1 << 20) * needed + jnp.arange(needed, dtype=jnp.int32)[None, :]
    picked = jnp.take_along_axis(picked, jnp.argsort(mixing, axis=1), axis=1)
    first = jax.random.randint(keys[3], (devices, needed), 0, DB_DEV)
    second = jax.random.randint(keys[4], (devices, needed), 0, DB_DEV)
    local_rows = first * second // DB_DEV
    picked = picked.reshape(devices * CH_DEV, 2)
    local_rows = local_rows.reshape(devices * CH_DEV, 2)
    clash = (picked[:, 0] == picked[:, 1]) & (local_rows[:, 0] == local_rows[:, 1])
    later = jnp.where(clash, (local_rows[:, 1] + 1) % DB_DEV, local_rows[:, 1])
    local_rows = jnp.stack([local_rows[:, 0], later], axis=1)
    return (picked * DB_DEV + local_rows).astype(jnp.int32)


def draw_database(key, part):
    keys = jax.random.split(jax.random.fold_in(key, 11), 1)
    base = jnp.clip(jax.random.normal(keys[0], (DB_SPANS, LEN, D), jnp.float32), -6.0, 6.0)
    return base.astype(jnp.bfloat16)


def steps_of(stream_key, dims, shards, smallest, high):
    gain, own = 1.0, jax.random.fold_in(stream_key, 6)
    for position, shards_of in shards:
        heights = jnp.exp(jax.random.uniform(jax.random.fold_in(own, position), (shards_of,), jnp.float32, smallest / len(shards), high / len(shards)))
        gain = gain * jnp.repeat(heights, dims[position] // shards_of).reshape([-1 if axis == position else 1 for axis in range(len(dims))])
    return gain


def bell_draw(key, dims, spread, limit, shards=(), kind=jnp.bfloat16):
    values = jax.random.normal(key, dims, jnp.float32) * spread
    if len(shards) > 0:
        values = steps_of(key, dims, shards, -0.22, 0.18) * values
    return jnp.clip(values, min=-limit, max=limit).astype(kind)


def setup_inputs(seed: int = 0) -> dict:
    arg_keys = jax.random.split(jax.random.key(seed), 9)
    tokens = bell_draw(arg_keys[0], (SPANS, LEN, D), 1.0, 6.0, ((0, 128),))
    neighbours = draw_neighbours(jax.random.fold_in(arg_keys[8], 71), 0)
    database = draw_database(jax.random.fold_in(arg_keys[8], 71), 0)
    norm_gain = jnp.clip(1.0 + 0.18 * jax.random.normal(arg_keys[3], (D,), jnp.float32), 0.1, 1.9)
    q_weight = bell_draw(arg_keys[4], (D, D), D ** -0.5, 0.1875, ((0, 128),))
    key_weight = bell_draw(arg_keys[5], (D, D), D ** -0.5, 0.1875, ((0, 128),))
    value_weight = bell_draw(arg_keys[6], (D, D), D ** -0.5, 0.1875, ((0, 128),))
    out_weight = bell_draw(arg_keys[7], (D, D), D ** -0.5, 0.1875, ((0, 128),))
    return dict(tokens=tokens, neighbours=neighbours, database=database, norm_gain=norm_gain, q_weight=q_weight, key_weight=key_weight, value_weight=value_weight, out_weight=out_weight)


def attend(queries, key_rows, value_rows):
    head_dim = D // HEADS
    scores = jnp.einsum('cihd,cnjhd->cnhij', queries.astype(jnp.float32), key_rows.astype(jnp.float32)) / math.sqrt(head_dim)
    row_peak = lax.optimization_barrier(jnp.max(scores, axis=-1, keepdims=True))
    exponent = jnp.exp(scores - row_peak)
    totals = lax.optimization_barrier(jnp.sum(exponent, axis=-1))
    probs = exponent.astype(jnp.bfloat16)
    partial_value = jnp.einsum('cnhij,cnjhd->cnhid', probs.astype(jnp.float32), value_rows.astype(jnp.float32))
    peaks = row_peak[..., 0]
    best_peak = lax.optimization_barrier(jnp.max(peaks, axis=1, keepdims=True))
    rescale = jnp.exp(peaks - best_peak)
    numerator = lax.optimization_barrier(jnp.sum(rescale[..., None] * partial_value, axis=1))
    denominator = lax.optimization_barrier(jnp.sum(rescale * totals, axis=1))
    attended = numerator / denominator[..., None]
    joined = jnp.transpose(attended, (0, 2, 1, 3))
    return joined.reshape(joined.shape[0], joined.shape[1], D).astype(jnp.bfloat16)

def reference(tokens, neighbours, database, norm_gain, q_weight, key_weight, value_weight, out_weight):
    groups = SPANS // CH_DEV
    head_dim = D // HEADS

    def process(pair):
        group_tokens, group_nbrs = pair
        floated = group_tokens.astype(jnp.float32)
        normed = (floated * lax.rsqrt(lax.optimization_barrier(jnp.mean(floated * floated, axis=-1, keepdims=True)) + 1e-05) * norm_gain).astype(jnp.bfloat16)
        queries = jnp.dot(normed.reshape(-1, D), q_weight, preferred_element_type=jnp.float32).astype(jnp.bfloat16)
        queries = queries.reshape(CH_DEV, LEN, HEADS, head_dim)
        fetched = database[group_nbrs.reshape(-1)].reshape(-1, D)
        key_rows = jnp.dot(fetched, key_weight, preferred_element_type=jnp.float32).astype(jnp.bfloat16)
        value_rows = jnp.dot(fetched, value_weight, preferred_element_type=jnp.float32).astype(jnp.bfloat16)
        key_rows = key_rows.reshape(CH_DEV, NEIGH, LEN, HEADS, head_dim)
        value_rows = value_rows.reshape(CH_DEV, NEIGH, LEN, HEADS, head_dim)
        attended = attend(queries, key_rows, value_rows)
        projected = jnp.dot(attended.reshape(-1, D), out_weight, preferred_element_type=jnp.float32)
        return (floated + projected.reshape(CH_DEV, LEN, D)).astype(jnp.bfloat16)
    result = lax.map(process, (tokens.reshape(groups, CH_DEV, LEN, D), neighbours.reshape(groups, CH_DEV, NEIGH)))
    return result.reshape(SPANS, LEN, D)
```

```python
import functools

import jax
import jax.numpy as jnp
from jax import lax
from jax.experimental import pallas as pl
from jax.experimental.pallas import tpu as pltpu
from jax.sharding import PartitionSpec as P

HEADS = 16
GROUP = 4
ANY = pl.ANY


def gather_kernel(rows_ref, table_ref, out_ref, held, in_sems, out_sems):
    count = held.shape[0]

    def read(i):
        return pltpu.make_async_copy(table_ref.at[rows_ref[i]], held.at[i], in_sems.at[i])

    def write(i):
        return pltpu.make_async_copy(held.at[i], out_ref.at[i], out_sems.at[i])

    for i in range(count):
        read(i).start()
    for i in range(count):
        read(i).wait()
        write(i).start()
    for i in range(count):
        write(i).wait()


def gather_rows(table, rows):
    count = rows.shape[0]
    shape = (count,) + table.shape[1:]
    nbytes = 2 * count * table.shape[1] * table.shape[2]
    return pl.pallas_call(
        gather_kernel,
        out_shape=jax.ShapeDtypeStruct(shape, table.dtype),
        grid_spec=pltpu.PrefetchScalarGridSpec(
            num_scalar_prefetch=1,
            grid=(1,),
            in_specs=[pl.BlockSpec(memory_space=ANY)],
            out_specs=pl.BlockSpec(memory_space=ANY),
            scratch_shapes=[
                pltpu.VMEM(shape, table.dtype),
                pltpu.SemaphoreType.DMA((count,)),
                pltpu.SemaphoreType.DMA((count,)),
            ],
        ),
        cost_estimate=pl.CostEstimate(flops=0, bytes_accessed=2 * nbytes, transcendentals=0),
    )(rows, table)


def query_kernel(tokens_ref, gain_ref, w_ref, out_ref):
    floated = tokens_ref[...].astype(jnp.float32)
    mean = jnp.mean(floated * floated, axis=-1, keepdims=True)
    normed = (floated * lax.rsqrt(mean + 1e-05) * gain_ref[...]).astype(jnp.bfloat16)
    out_ref[...] = jnp.dot(normed, w_ref[...], preferred_element_type=jnp.float32).astype(
        jnp.bfloat16
    )


def project_queries(flat, gain, weights, tile=256):
    rows, width = flat.shape
    return pl.pallas_call(
        query_kernel,
        out_shape=jax.ShapeDtypeStruct((rows, width), jnp.bfloat16),
        grid=(rows // tile,),
        in_specs=[
            pl.BlockSpec((tile, width), lambda i: (i, 0)),
            pl.BlockSpec((1, width), lambda i: (0, 0)),
            pl.BlockSpec((width, width), lambda i: (0, 0)),
        ],
        out_specs=pl.BlockSpec((tile, width), lambda i: (i, 0)),
        cost_estimate=pl.CostEstimate(
            flops=2 * rows * width * width, bytes_accessed=6 << 20, transcendentals=0
        ),
    )(flat, gain, weights)


def keys_kernel(blocks_ref, w_key_ref, w_value_ref, out_ref):
    width = blocks_ref.shape[1]
    blocks = blocks_ref[...]
    out_ref[:, :width] = jnp.dot(
        blocks, w_key_ref[...], preferred_element_type=jnp.float32
    ).astype(jnp.bfloat16)
    out_ref[:, width:] = jnp.dot(
        blocks, w_value_ref[...], preferred_element_type=jnp.float32
    ).astype(jnp.bfloat16)


def project_blocks(flat, weights, tile=256):
    rows, width = flat.shape
    return pl.pallas_call(
        keys_kernel,
        out_shape=jax.ShapeDtypeStruct((rows, 2 * width), jnp.bfloat16),
        grid=(rows // tile,),
        in_specs=[
            pl.BlockSpec((tile, width), lambda i: (i, 0)),
            pl.BlockSpec((width, width), lambda i: (0, 1)),
            pl.BlockSpec((width, width), lambda i: (0, 2)),
        ],
        out_specs=pl.BlockSpec((tile, 2 * width), lambda i: (i, 0)),
        cost_estimate=pl.CostEstimate(
            flops=4 * rows * width * width, bytes_accessed=16 << 20, transcendentals=0
        ),
    )(flat, weights, weights)


def tail_kernel(
    holders,
    extra,
    length,
    meta_ref,
    tokens_ref,
    queries_ref,
    w_key_ref,
    w_value_ref,
    w_out_ref,
    first_ref,
    second_ref,
    out_ref,
    rows_held,
    blocks_held,
    joined,
    rows_sem,
    block_sems,
):
    step = pl.program_id(0)
    width = tokens_ref.shape[1]
    spans = tokens_ref.shape[0] // length
    lanes_n = GROUP * (width // HEADS)
    n_second = meta_ref[2 * holders]

    @pl.when(step == 0)
    def _():
        first = pltpu.make_async_copy(first_ref, rows_held.at[pl.ds(0, holders)], rows_sem)

        def read(i):
            return pltpu.make_async_copy(
                second_ref.at[meta_ref[holders + i]],
                blocks_held.at[pl.ds(i * length, length)],
                block_sems.at[i],
            )

        for i in range(extra):
            read(i).start()
        first.start()
        for i in range(extra):
            read(i).wait()
        for t in range(extra // 4):

            @pl.when(n_second > 4 * t)
            def _():
                blocks = blocks_held[4 * t * length : 4 * (t + 1) * length, :]
                for at, w_ref in ((0, w_key_ref), (width, w_value_ref)):
                    rows = jnp.dot(
                        blocks, w_ref[...], preferred_element_type=jnp.float32
                    ).astype(jnp.bfloat16)
                    rows_held[holders + 4 * t : holders + 4 * t + 4, :, at : at + width] = (
                        rows.reshape(4, length, width)
                    )

        first.wait()

    lane = lax.broadcasted_iota(jnp.int32, (1, lanes_n), 1) // (width // HEADS)

    def span(c, _):
        at = (step * spans + c) * 2
        one, two = meta_ref[at], meta_ref[at + 1]
        row = pl.multiple_of(c * length, length)
        for g in range(HEADS // GROUP):
            cols = slice(g * lanes_n, (g + 1) * lanes_n)
            vcols = slice(width + g * lanes_n, width + (g + 1) * lanes_n)
            queries = queries_ref[pl.ds(row, length), cols].astype(jnp.float32)
            stacked = jnp.concatenate(
                [jnp.where(lane == h, queries, 0.0) for h in range(GROUP)], axis=0
            ).astype(jnp.bfloat16)
            keys = jnp.concatenate([rows_held[one, :, cols], rows_held[two, :, cols]], axis=0)
            values = jnp.concatenate(
                [rows_held[one, :, vcols], rows_held[two, :, vcols]], axis=0
            )
            scores = lax.dot_general(
                stacked, keys, (((1,), (1,)), ((), ())), preferred_element_type=jnp.float32
            ) * ((width // HEADS) ** -0.5)
            peak = jnp.max(scores, axis=-1, keepdims=True)
            exponent = jnp.exp(scores - peak)
            totals = jnp.sum(exponent, axis=-1, keepdims=True)
            summed = jnp.dot(
                exponent.astype(jnp.bfloat16), values, preferred_element_type=jnp.float32
            ) / totals
            attended = summed[:length]
            for h in range(1, GROUP):
                attended = jnp.where(
                    lane == h, summed[h * length : (h + 1) * length], attended
                )
            joined[pl.ds(row, length), cols] = attended.astype(jnp.bfloat16)
        return _

    lax.fori_loop(0, spans, span, 0)
    projected = jnp.dot(joined[...], w_out_ref[...], preferred_element_type=jnp.float32)
    out_ref[...] = (tokens_ref[...].astype(jnp.float32) + projected).astype(jnp.bfloat16)


def finish(meta, flat, queries, weights, first, second, holders, extra, length, spans=4):
    rows, width = flat.shape
    tile = spans * length
    resident = pl.Buffered(1)
    return pl.pallas_call(
        functools.partial(tail_kernel, holders, extra, length),
        out_shape=jax.ShapeDtypeStruct((rows, width), jnp.bfloat16),
        grid_spec=pltpu.PrefetchScalarGridSpec(
            num_scalar_prefetch=1,
            grid=(rows // tile,),
            in_specs=[
                pl.BlockSpec((tile, width), lambda i, m: (i, 0)),
                pl.BlockSpec((tile, width), lambda i, m: (i, 0)),
                pl.BlockSpec((width, width), lambda i, m: (0, 1), pipeline_mode=resident),
                pl.BlockSpec((width, width), lambda i, m: (0, 2), pipeline_mode=resident),
                pl.BlockSpec((width, width), lambda i, m: (0, 3), pipeline_mode=resident),
                pl.BlockSpec(memory_space=ANY),
                pl.BlockSpec(memory_space=ANY),
            ],
            out_specs=pl.BlockSpec((tile, width), lambda i, m: (i, 0)),
            scratch_shapes=[
                pltpu.VMEM((holders + extra, length, 2 * width), jnp.bfloat16),
                pltpu.VMEM((extra * length, width), jnp.bfloat16),
                pltpu.VMEM((tile, width), jnp.bfloat16),
                pltpu.SemaphoreType.DMA,
                pltpu.SemaphoreType.DMA((extra,)),
            ],
        ),
        compiler_params=pltpu.CompilerParams(vmem_limit_bytes=48 << 20),
        cost_estimate=pl.CostEstimate(
            flops=15 << 30, bytes_accessed=24 << 20, transcendentals=2 << 20
        ),
    )(meta, flat, queries, weights, weights, weights, first, second)


def shards(tokens, neighbours, database, norm_gain, q_weight, key_weight, value_weight, out_weight):
    spans, length, width = tokens.shape
    holders = lax.axis_size("db")
    slab = database.shape[0]
    shard = jnp.concatenate([q_weight, key_weight, value_weight, out_weight], axis=1)
    weights = lax.all_gather(shard, ("dp", "db"), axis=0, tiled=True)

    wanted_ids = neighbours.reshape(-1)
    needed = wanted_ids.shape[0]
    extra = needed // 2
    holder_of = wanted_ids // slab
    local_row = wanted_ids % slab
    position = jnp.arange(needed, dtype=jnp.int32)
    earlier = position[None, :] < position[:, None]
    same = holder_of[None, :] == holder_of[:, None]
    rank_of = jnp.sum((same & earlier).astype(jnp.int32), axis=1)
    slot_of = rank_of * holders + holder_of
    hit = slot_of[:, None] == jnp.arange(2 * holders, dtype=jnp.int32)[None, :]
    wanted = jnp.sum(jnp.where(hit, local_row[:, None], 0), axis=0).reshape(2, holders)
    incoming = lax.all_to_all(wanted, "db", split_axis=1, concat_axis=1, tiled=True)
    rows = jnp.clip(incoming, 0, slab - 1)
    first = lax.all_to_all(
        gather_rows(database, rows[0]), "db", split_axis=0, concat_axis=0, tiled=True
    )
    second = lax.all_to_all(
        gather_rows(database, rows[1]), "db", split_axis=0, concat_axis=0, tiled=True
    )

    extra_of = jnp.sum(jnp.where(earlier, rank_of[None, :], 0), axis=1)
    place = jnp.where(rank_of == 0, holder_of, holders + extra_of)
    chosen = (rank_of[:, None] == 1) & (
        extra_of[:, None] == jnp.arange(extra, dtype=jnp.int32)[None, :]
    )
    extras = jnp.sum(jnp.where(chosen, holder_of[:, None], 0), axis=0)
    meta = jnp.concatenate(
        [place, extras, jnp.zeros((holders - extra,), jnp.int32), jnp.sum(rank_of)[None]]
    )

    flat = tokens.reshape(-1, width)
    queries = project_queries(flat, norm_gain.reshape(1, -1), weights)
    first_rows = project_blocks(first.reshape(-1, width), weights)
    mixed = finish(
        meta,
        flat,
        queries,
        weights,
        first_rows.reshape(holders, length, 2 * width),
        second,
        holders,
        extra,
        length,
    )
    return mixed.reshape(tokens.shape)


def solution(mesh):
    both = P(("dp", "db"), None)
    placed = (
        P(("dp", "db"), None, None),
        both,
        P("db", None, None),
        P(),
        both,
        both,
        both,
        both,
    )
    return jax.shard_map(
        shards, mesh=mesh, in_specs=placed, out_specs=P(("dp", "db"), None, None), check_vma=False
    )
```

```python
import functools

import jax
import jax.numpy as jnp
from jax import lax
from jax.experimental import pallas as pl
from jax.experimental.pallas import tpu as pltpu
from jax.sharding import PartitionSpec as P


HEADS = 16
GROUP = 4
ANY = pl.ANY
HBM = pltpu.MemorySpace.HBM


def gather_kernel(rows_ref, table_ref, out_ref, held, in_sems, out_sems):
    count = held.shape[0]

    def read(i):
        return pltpu.make_async_copy(table_ref.at[rows_ref[i]], held.at[i], in_sems.at[i])

    def write(i):
        return pltpu.make_async_copy(held.at[i], out_ref.at[i], out_sems.at[i])

    for i in range(count):
        read(i).start()
    for i in range(count):
        read(i).wait()
        write(i).start()
    for i in range(count):
        write(i).wait()


def gather_rows(table, rows):
    count = rows.shape[0]
    shape = (count,) + table.shape[1:]
    nbytes = 2 * count * table.shape[1] * table.shape[2]
    return pl.pallas_call(
        gather_kernel,
        out_shape=jax.ShapeDtypeStruct(shape, table.dtype),
        grid_spec=pltpu.PrefetchScalarGridSpec(
            num_scalar_prefetch=1,
            grid=(1,),
            in_specs=[pl.BlockSpec(memory_space=ANY)],
            out_specs=pl.BlockSpec(memory_space=ANY),
            scratch_shapes=[
                pltpu.VMEM(shape, table.dtype),
                pltpu.SemaphoreType.DMA((count,)),
                pltpu.SemaphoreType.DMA((count,)),
            ],
        ),
        cost_estimate=pl.CostEstimate(flops=0, bytes_accessed=2 * nbytes, transcendentals=0),
    )(rows, table)


def assemble_kernel(size, core_ref, *refs):
    n = (len(refs) - 4) // 2
    mine, theirs = refs[:n], refs[n : 2 * n]
    out_ref, held, in_sems, out_sems = refs[2 * n :]
    core, me = core_ref[0], core_ref[1]
    rows, half = mine[0].shape
    starts = [(me, 0), (lax.rem(me + size - 1, size), 0), (lax.rem(me + 1, size), 0)]
    starts += [(lax.rem(me + 2, size), 0), (lax.rem(me + 2, size), rows // 2)]
    copies = []
    for s, (side, source) in enumerate(((core, mine), (1 - core, theirs))):
        for i, ref in enumerate(source):
            piece, within = starts[i]
            height = ref.shape[0]
            at = pl.multiple_of(piece * rows + within, 16)
            left = pl.multiple_of(side * half, 128)
            spot = held.at[s, pl.ds(at, height)]
            read = pltpu.make_async_copy(ref, spot, in_sems.at[s * n + i])
            write = pltpu.make_async_copy(
                spot, out_ref.at[pl.ds(at, height), pl.ds(left, half)], out_sems.at[s * n + i]
            )
            copies.append((read, write))
    for read, _ in copies:
        read.start()
    for read, write in copies:
        read.wait()
        write.start()
    for _, write in copies:
        write.wait()


def assemble(where, mine, theirs, size):
    rows, half = mine[0].shape
    n = len(mine)
    return pl.pallas_call(
        functools.partial(assemble_kernel, size),
        out_shape=jax.ShapeDtypeStruct((size * rows, 2 * half), mine[0].dtype),
        grid_spec=pltpu.PrefetchScalarGridSpec(
            num_scalar_prefetch=1,
            grid=(1,),
            in_specs=[pl.BlockSpec(memory_space=ANY)] * (2 * n),
            out_specs=pl.BlockSpec(memory_space=ANY),
            scratch_shapes=[
                pltpu.VMEM((2, size * rows, half), mine[0].dtype),
                pltpu.SemaphoreType.DMA((2 * n,)),
                pltpu.SemaphoreType.DMA((2 * n,)),
            ],
        ),
        cost_estimate=pl.CostEstimate(flops=0, bytes_accessed=16 << 20, transcendentals=0),
    )(where, *mine, *theirs)


def query_kernel(tokens_ref, gain_ref, w_ref, out_ref):
    floated = tokens_ref[...].astype(jnp.float32)
    mean = jnp.mean(floated * floated, axis=-1, keepdims=True)
    normed = (floated * lax.rsqrt(mean + 1e-05) * gain_ref[...]).astype(jnp.bfloat16)
    out_ref[...] = jnp.dot(normed, w_ref[...], preferred_element_type=jnp.float32).astype(
        jnp.bfloat16
    )


def project_queries(flat, gain, weights, tile=256):
    rows, width = flat.shape
    return pl.pallas_call(
        query_kernel,
        out_shape=jax.ShapeDtypeStruct((rows, width), jnp.bfloat16),
        grid=(rows // tile,),
        in_specs=[
            pl.BlockSpec((tile, width), lambda i: (i, 0)),
            pl.BlockSpec((1, width), lambda i: (0, 0)),
            pl.BlockSpec((width, width), lambda i: (0, 0)),
        ],
        out_specs=pl.BlockSpec((tile, width), lambda i: (i, 0)),
        cost_estimate=pl.CostEstimate(
            flops=2 * rows * width * width, bytes_accessed=6 << 20, transcendentals=0
        ),
    )(flat, gain, weights)


def attend(lane, queries, one, two, rows_held, joined, row):
    length, width = queries.shape
    head = width // HEADS
    lanes_n = GROUP * head
    for g in range(HEADS // GROUP):
        cols = slice(g * lanes_n, (g + 1) * lanes_n)
        vcols = slice(width + g * lanes_n, width + (g + 1) * lanes_n)
        part = queries[:, cols].astype(jnp.float32)
        stacked = jnp.concatenate(
            [jnp.where(lane == h, part, 0.0) for h in range(GROUP)], axis=0
        ).astype(jnp.bfloat16)
        keys = jnp.concatenate([rows_held[one, :, cols], rows_held[two, :, cols]], axis=0)
        values = jnp.concatenate([rows_held[one, :, vcols], rows_held[two, :, vcols]], axis=0)
        scores = lax.dot_general(
            stacked, keys, (((1,), (1,)), ((), ())), preferred_element_type=jnp.float32
        ) * (head**-0.5)
        peak = jnp.max(scores, axis=-1, keepdims=True)
        exponent = jnp.exp(scores - peak)
        totals = jnp.sum(exponent, axis=-1, keepdims=True)
        summed = (
            jnp.dot(exponent.astype(jnp.bfloat16), values, preferred_element_type=jnp.float32)
            / totals
        )
        attended = summed[:length]
        for h in range(1, GROUP):
            attended = jnp.where(lane == h, summed[h * length : (h + 1) * length], attended)
        joined[pl.ds(row, length), cols] = attended.astype(jnp.bfloat16)


def project_rows(blocks, w_held, rows_held, first, width):
    count = blocks.shape[0] // rows_held.shape[1]
    for at in (0, width):
        rows = jnp.dot(
            blocks, w_held[:, at : at + width], preferred_element_type=jnp.float32
        ).astype(jnp.bfloat16)
        rows_held[pl.ds(first, count), :, at : at + width] = rows.reshape(
            count, rows_held.shape[1], width
        )


class Spans:
    def __init__(self, meta_ref, slots, held, out_ref, out_sems):
        self.meta_ref, self.slots, self.held = meta_ref, slots, held
        self.out_ref, self.out_sems = out_ref, out_sems

    def span_at(self, position):
        return self.meta_ref[self.slots + position]

    def write(self, position):
        return pltpu.make_async_copy(
            self.held["out"].at[position],
            self.out_ref.at[self.span_at(position)],
            self.out_sems.at[position],
        )

    def step(self, group, live, load):
        held, meta_ref = self.held, self.meta_ref
        length, width = held["tokens"].shape[1:]
        lane = lax.broadcasted_iota(jnp.int32, (1, GROUP * (width // HEADS)), 1) // (
            width // HEADS
        )

        def span(t, _):
            position = group * 4 + t

            @pl.when(live(position))
            def _():
                load(position)
                c = self.span_at(position)
                attend(
                    lane,
                    held["queries"][c],
                    meta_ref[2 * c],
                    meta_ref[2 * c + 1],
                    held["rows"],
                    held["joined"],
                    pl.multiple_of(t * length, length),
                )

            return 0

        lax.fori_loop(0, 4, span, 0)
        projected = jnp.dot(
            held["joined"][...], held["w_out"][...], preferred_element_type=jnp.float32
        )
        for t in range(4):
            position = group * 4 + t

            @pl.when(live(position))
            def _():
                c = self.span_at(position)
                held["out"][position] = (
                    held["tokens"][c].astype(jnp.float32)
                    + projected[t * length : (t + 1) * length]
                ).astype(jnp.bfloat16)
                self.write(position).start()


def first_kernel(
    slots,
    meta_ref,
    tokens_ref,
    queries_ref,
    weights_ref,
    blocks_ref,
    rows_ref,
    out_ref,
    tokens_held,
    queries_held,
    w_held,
    w_out_held,
    blocks_held,
    rows_held,
    joined,
    out_held,
    in_sems,
    block_sems,
    row_sems,
    out_sems,
):
    spans, length, width = tokens_held.shape
    n_late = meta_ref[slots + spans]
    tile = 4
    tiles = blocks_held.shape[0] // tile
    loads = [
        pltpu.make_async_copy(
            weights_ref.at[:, pl.ds(width, 2 * width)], w_held, in_sems.at[0]
        ),
        pltpu.make_async_copy(
            weights_ref.at[:, pl.ds(3 * width, width)], w_out_held, in_sems.at[1]
        ),
        pltpu.make_async_copy(queries_ref, queries_held, in_sems.at[2]),
        pltpu.make_async_copy(tokens_ref, tokens_held, in_sems.at[3]),
    ]

    def block(i):
        at = pl.ds(pl.multiple_of(i * tile, tile), tile)
        return pltpu.make_async_copy(blocks_ref.at[at], blocks_held.at[at], block_sems.at[i])

    def row(i):
        at = pl.ds(pl.multiple_of(i * tile, tile), tile)
        return pltpu.make_async_copy(rows_held.at[at], rows_ref.at[at], row_sems.at[i])

    block(0).start()
    loads[0].start()
    for i in range(1, tiles):
        block(i).start()
    for load in loads[1:]:
        load.start()
    loads[0].wait()

    def keys(i, _):
        block(i).wait()
        first = pl.multiple_of(i * tile, tile)
        blocks = blocks_held[pl.ds(first, tile)].reshape(tile * length, width)
        project_rows(blocks, w_held, rows_held, first, width)
        row(i).start()
        return 0

    lax.fori_loop(0, tiles, keys, 0)
    for load in loads[1:]:
        load.wait()
    held = dict(
        tokens=tokens_held,
        queries=queries_held,
        rows=rows_held,
        joined=joined,
        w_out=w_out_held,
        out=out_held,
    )
    work = Spans(meta_ref, slots, held, out_ref, out_sems)

    def live(position):
        return position >= n_late

    for group in range(spans // 4):

        @pl.when(live(4 * group + 3))
        def _():
            work.step(group, live, lambda position: None)

    for position in range(spans):

        @pl.when(live(position))
        def _():
            work.write(position).wait()

    for i in range(tiles):
        row(i).wait()


def last_kernel(
    slots,
    holders,
    meta_ref,
    tokens_ref,
    queries_ref,
    weights_ref,
    rows_ref,
    second_ref,
    early_ref,
    out_ref,
    tokens_held,
    queries_held,
    w_held,
    w_out_held,
    blocks_held,
    rows_held,
    joined,
    out_held,
    in_sems,
    block_sems,
    span_sems,
    row_sems,
    out_sems,
):
    del early_ref
    spans, length, width = tokens_held.shape
    extra = blocks_held.shape[0]
    n_late = meta_ref[slots + spans]
    n_extra = meta_ref[slots + spans + 1]
    loads = [
        pltpu.make_async_copy(
            weights_ref.at[:, pl.ds(width, 2 * width)], w_held, in_sems.at[0]
        ),
        pltpu.make_async_copy(
            weights_ref.at[:, pl.ds(3 * width, width)], w_out_held, in_sems.at[1]
        ),
    ]

    def block(i):
        return pltpu.make_async_copy(
            second_ref.at[meta_ref[slots + spans + 2 + i]], blocks_held.at[i], block_sems.at[i]
        )

    def span_loads(position):
        c = meta_ref[slots + position]
        return (
            pltpu.make_async_copy(
                queries_ref.at[c], queries_held.at[c], span_sems.at[0, position]
            ),
            pltpu.make_async_copy(
                tokens_ref.at[c], tokens_held.at[c], span_sems.at[1, position]
            ),
        )

    def early_rows(position, n):
        p = meta_ref[2 * meta_ref[slots + position] + n]
        copy = pltpu.make_async_copy(
            rows_ref.at[jnp.minimum(p, holders - 1)],
            rows_held.at[jnp.minimum(p, holders - 1)],
            row_sems.at[n, position],
        )
        return p < holders, copy

    for i in range(extra):

        @pl.when(i < n_extra)
        def _():
            block(i).start()

    for load in loads:
        load.start()

    def start(position, _):
        @pl.when(position < n_late)
        def _():
            for copy in span_loads(position):
                copy.start()
            for n in range(2):
                early, copy = early_rows(position, n)

                @pl.when(early)
                def _():
                    copy.start()

        return 0

    lax.fori_loop(0, spans, start, 0)
    for i in range(extra):

        @pl.when(i < n_extra)
        def _():
            block(i).wait()

    loads[0].wait()
    for t in range(extra // 4):

        @pl.when(4 * t < n_extra)
        def _():
            blocks = blocks_held[4 * t : 4 * t + 4].reshape(4 * length, width)
            project_rows(blocks, w_held, rows_held, holders + 4 * t, width)

    loads[1].wait()
    held = dict(
        tokens=tokens_held,
        queries=queries_held,
        rows=rows_held,
        joined=joined,
        w_out=w_out_held,
        out=out_held,
    )
    work = Spans(meta_ref, slots, held, out_ref, out_sems)

    def live(position):
        return position < n_late

    def load(position):
        for copy in span_loads(position):
            copy.wait()
        for n in range(2):
            early, copy = early_rows(position, n)

            @pl.when(early)
            def _():
                copy.wait()

    for group in range(spans // 4):

        @pl.when(live(4 * group))
        def _():
            work.step(group, live, load)

    for position in range(spans):

        @pl.when(live(position))
        def _():
            work.write(position).wait()


def project_first(meta, tokens, queries, weights, first):
    spans, length, width = tokens.shape
    holders = first.shape[0]
    kind = tokens.dtype
    anywhere = pl.BlockSpec(memory_space=HBM)
    return pl.pallas_call(
        functools.partial(first_kernel, 2 * spans),
        out_shape=(
            jax.ShapeDtypeStruct((holders, length, 2 * width), kind),
            jax.ShapeDtypeStruct(tokens.shape, kind),
        ),
        grid_spec=pltpu.PrefetchScalarGridSpec(
            num_scalar_prefetch=1,
            grid=(1,),
            in_specs=[anywhere] * 4,
            out_specs=(anywhere, anywhere),
            scratch_shapes=[
                pltpu.VMEM(tokens.shape, kind),
                pltpu.VMEM(tokens.shape, kind),
                pltpu.VMEM((width, 2 * width), kind),
                pltpu.VMEM((width, width), kind),
                pltpu.VMEM(first.shape, kind),
                pltpu.VMEM((holders, length, 2 * width), kind),
                pltpu.VMEM((4 * length, width), kind),
                pltpu.VMEM(tokens.shape, kind),
                pltpu.SemaphoreType.DMA((4,)),
                pltpu.SemaphoreType.DMA((holders // 4,)),
                pltpu.SemaphoreType.DMA((holders // 4,)),
                pltpu.SemaphoreType.DMA((spans,)),
            ],
        ),
        compiler_params=pltpu.CompilerParams(vmem_limit_bytes=48 << 20),
        cost_estimate=pl.CostEstimate(
            flops=15 << 30, bytes_accessed=32 << 20, transcendentals=1 << 20
        ),
    )(meta, tokens, queries, weights, first)


def finish(meta, tokens, queries, weights, first_rows, second, early):
    spans, length, width = tokens.shape
    holders = first_rows.shape[0]
    extra = spans
    kind = tokens.dtype
    anywhere = pl.BlockSpec(memory_space=HBM)
    return pl.pallas_call(
        functools.partial(last_kernel, 2 * spans, holders),
        out_shape=jax.ShapeDtypeStruct(tokens.shape, kind),
        grid_spec=pltpu.PrefetchScalarGridSpec(
            num_scalar_prefetch=1,
            grid=(1,),
            in_specs=[anywhere] * 6,
            out_specs=anywhere,
            scratch_shapes=[
                pltpu.VMEM(tokens.shape, kind),
                pltpu.VMEM(tokens.shape, kind),
                pltpu.VMEM((width, 2 * width), kind),
                pltpu.VMEM((width, width), kind),
                pltpu.VMEM((extra, length, width), kind),
                pltpu.VMEM((holders + extra, length, 2 * width), kind),
                pltpu.VMEM((4 * length, width), kind),
                pltpu.VMEM(tokens.shape, kind),
                pltpu.SemaphoreType.DMA((2,)),
                pltpu.SemaphoreType.DMA((extra,)),
                pltpu.SemaphoreType.DMA((2, spans)),
                pltpu.SemaphoreType.DMA((2, spans)),
                pltpu.SemaphoreType.DMA((spans,)),
            ],
        ),
        input_output_aliases={6: 0},
        compiler_params=pltpu.CompilerParams(vmem_limit_bytes=48 << 20),
        cost_estimate=pl.CostEstimate(
            flops=8 << 30, bytes_accessed=16 << 20, transcendentals=1 << 20
        ),
    )(meta, tokens, queries, weights, first_rows, second, early)


def shards(tokens, neighbours, database, norm_gain, q_weight, key_weight, value_weight, out_weight):
    spans, length, width = tokens.shape
    holders = lax.axis_size("db")
    slab = database.shape[0]
    wanted_ids = neighbours.reshape(-1)
    needed = wanted_ids.shape[0]
    extra = needed // 2
    holder_of = wanted_ids // slab
    local_row = wanted_ids % slab
    position = jnp.arange(needed, dtype=jnp.int32)
    earlier = position[None, :] < position[:, None]
    same = holder_of[None, :] == holder_of[:, None]
    rank_of = jnp.sum((same & earlier).astype(jnp.int32), axis=1)
    slot_of = rank_of * holders + holder_of
    hit = slot_of[:, None] == jnp.arange(2 * holders, dtype=jnp.int32)[None, :]
    wanted = jnp.sum(jnp.where(hit, local_row[:, None], 0), axis=0).reshape(2, holders)
    halves = jnp.stack(
        [
            jnp.concatenate([q_weight, key_weight], axis=1),
            jnp.concatenate([value_weight, out_weight], axis=1),
        ]
    )
    height, half = halves.shape[1:]
    ask = jnp.pad(
        wanted.T.astype(jnp.bfloat16)[:, None, :], ((0, 0), (0, height - 1), (0, 126))
    )
    parcels = jnp.concatenate([jnp.tile(halves, (holders // 2, 1, 1)), ask], axis=2)
    arrived = lax.all_to_all(parcels, "db", split_axis=0, concat_axis=0, tiled=True)
    incoming = arrived[:, 0, half : half + 2].T.astype(jnp.int32)
    rows = jnp.clip(incoming, 0, slab - 1)
    picked = gather_rows(database, rows[0])
    first = lax.all_to_all(picked, "db", split_axis=0, concat_axis=0, tiled=True)
    own = arrived[:, :, :half].reshape(holders * height, half)
    own, _ = lax.optimization_barrier((own, picked))
    size = lax.axis_size("dp")
    before = [(i, (i + 1) % size) for i in range(size)]
    after = [(i, (i + size - 1) % size) for i in range(size)]
    middle = own.shape[0] // 2
    left = lax.ppermute(own, "dp", before)
    right = lax.ppermute(own, "dp", after)
    late_rows, left, right = lax.optimization_barrier((rows[1], left, right))
    far_top = lax.ppermute(left[:middle], "dp", before)
    far_bottom = lax.ppermute(right[middle:], "dp", after)
    late, far_top, far_bottom = lax.optimization_barrier(
        (gather_rows(database, late_rows), far_top, far_bottom)
    )
    second = lax.all_to_all(late, "db", split_axis=0, concat_axis=0, tiled=True)
    mine = [own, left, right, far_top, far_bottom]
    swap = [(i, i ^ 1) for i in range(holders)]
    theirs = [lax.ppermute(piece, "db", swap) for piece in mine]
    where = jnp.stack([lax.axis_index("db") % 2, lax.axis_index("dp")]).astype(jnp.int32)
    weights = assemble(where, mine, theirs, size)

    extra_of = jnp.sum(jnp.where(earlier, rank_of[None, :], 0), axis=1)
    place = jnp.where(rank_of == 0, holder_of, holders + extra_of)
    chosen = (rank_of[:, None] == 1) & (
        extra_of[:, None] == jnp.arange(extra, dtype=jnp.int32)[None, :]
    )
    extras = jnp.sum(jnp.where(chosen, holder_of[:, None], 0), axis=0)
    span = jnp.arange(spans, dtype=jnp.int32)
    is_late = jnp.max(rank_of.reshape(spans, 2), axis=1)
    n_late = jnp.sum(is_late)
    late_before = jnp.sum(jnp.where(span[None, :] < span[:, None], is_late[None, :], 0), axis=1)
    listed = jnp.where(is_late == 1, late_before, n_late + span - late_before)
    order = jnp.sum(jnp.where(listed[:, None] == span[None, :], span[:, None], 0), axis=0)
    meta = jnp.concatenate([place, order, n_late[None], jnp.sum(rank_of)[None], extras])

    queries = project_queries(
        tokens.reshape(-1, width), norm_gain.reshape(1, -1), weights
    ).reshape(tokens.shape)
    first_rows, early = project_first(meta, tokens, queries, weights, first)
    return finish(meta, tokens, queries, weights, first_rows, second, early)


def solution(mesh):
    both = P(("dp", "db"), None)
    placed = (
        P(("dp", "db"), None, None),
        both,
        P("db", None, None),
        P(),
        both,
        both,
        both,
        both,
    )
    return jax.shard_map(
        shards, mesh=mesh, in_specs=placed, out_specs=P(("dp", "db"), None, None), check_vma=False
    )
```

```python
import functools
import math

import jax
import jax.numpy as jnp
from jax import lax
from jax.experimental import pallas as pl
from jax.experimental.pallas import tpu as pltpu
from jax.sharding import PartitionSpec as P


HEADS = 16
GROUP = 2
ANY = pl.ANY
HBM = pltpu.MemorySpace.HBM


def gather_kernel(rows_ref, table_ref, out_ref, held, in_sems, out_sems):
    count = held.shape[0]

    def read(i):
        return pltpu.make_async_copy(table_ref.at[rows_ref[i]], held.at[i], in_sems.at[i])

    def write(i):
        return pltpu.make_async_copy(held.at[i], out_ref.at[i], out_sems.at[i])

    for i in range(count):
        read(i).start()
    for i in range(count):
        read(i).wait()
        write(i).start()
    for i in range(count):
        write(i).wait()


def gather_rows(table, rows):
    count = rows.shape[0]
    shape = (count,) + table.shape[1:]
    nbytes = 2 * count * table.shape[1] * table.shape[2]
    return pl.pallas_call(
        gather_kernel,
        out_shape=jax.ShapeDtypeStruct(shape, table.dtype),
        grid_spec=pltpu.PrefetchScalarGridSpec(
            num_scalar_prefetch=1,
            grid=(1,),
            in_specs=[pl.BlockSpec(memory_space=ANY)],
            out_specs=pl.BlockSpec(memory_space=ANY),
            scratch_shapes=[
                pltpu.VMEM(shape, table.dtype),
                pltpu.SemaphoreType.DMA((count,)),
                pltpu.SemaphoreType.DMA((count,)),
            ],
        ),
        cost_estimate=pl.CostEstimate(flops=0, bytes_accessed=2 * nbytes, transcendentals=0),
    )(rows, table)


def assemble_kernel(size, core_ref, *refs):
    n = (len(refs) - 4) // 2
    mine, theirs = refs[:n], refs[n : 2 * n]
    out_ref, held, in_sems, out_sems = refs[2 * n :]
    core, me = core_ref[0], core_ref[1]
    rows, half = mine[0].shape
    starts = [(me, 0), (lax.rem(me + size - 1, size), 0), (lax.rem(me + 1, size), 0)]
    starts += [(lax.rem(me + 2, size), 0), (lax.rem(me + 2, size), rows // 2)]
    copies = []
    for s, (side, source) in enumerate(((core, mine), (1 - core, theirs))):
        for i, ref in enumerate(source):
            piece, within = starts[i]
            height = ref.shape[0]
            at = pl.multiple_of(piece * rows + within, 16)
            left = pl.multiple_of(side * half, 128)
            spot = held.at[s, pl.ds(at, height)]
            read = pltpu.make_async_copy(ref, spot, in_sems.at[s * n + i])
            write = pltpu.make_async_copy(
                spot, out_ref.at[pl.ds(at, height), pl.ds(left, half)], out_sems.at[s * n + i]
            )
            copies.append((read, write))
    for read, _ in copies:
        read.start()
    for read, write in copies:
        read.wait()
        write.start()
    for _, write in copies:
        write.wait()


def assemble(where, mine, theirs, size):
    rows, half = mine[0].shape
    n = len(mine)
    return pl.pallas_call(
        functools.partial(assemble_kernel, size),
        out_shape=jax.ShapeDtypeStruct((size * rows, 2 * half), mine[0].dtype),
        grid_spec=pltpu.PrefetchScalarGridSpec(
            num_scalar_prefetch=1,
            grid=(1,),
            in_specs=[pl.BlockSpec(memory_space=ANY)] * (2 * n),
            out_specs=pl.BlockSpec(memory_space=ANY),
            scratch_shapes=[
                pltpu.VMEM((2, size * rows, half), mine[0].dtype),
                pltpu.SemaphoreType.DMA((2 * n,)),
                pltpu.SemaphoreType.DMA((2 * n,)),
            ],
        ),
        cost_estimate=pl.CostEstimate(flops=0, bytes_accessed=16 << 20, transcendentals=0),
    )(where, *mine, *theirs)


def query_kernel(tokens_ref, gain_ref, w_ref, out_ref):
    floated = tokens_ref[...].astype(jnp.float32)
    mean = jnp.mean(floated * floated, axis=-1, keepdims=True)
    normed = (floated * lax.rsqrt(mean + 1e-05) * gain_ref[...]).astype(jnp.bfloat16)
    out_ref[...] = jnp.dot(normed, w_ref[...], preferred_element_type=jnp.float32).astype(
        jnp.bfloat16
    )


def project_queries(flat, gain, weights, tile=256):
    rows, width = flat.shape
    return pl.pallas_call(
        query_kernel,
        out_shape=jax.ShapeDtypeStruct((rows, width), jnp.bfloat16),
        grid=(rows // tile,),
        in_specs=[
            pl.BlockSpec((tile, width), lambda i: (i, 0)),
            pl.BlockSpec((1, width), lambda i: (0, 0)),
            pl.BlockSpec((width, width), lambda i: (0, 0)),
        ],
        out_specs=pl.BlockSpec((tile, width), lambda i: (i, 0)),
        cost_estimate=pl.CostEstimate(
            flops=2 * rows * width * width, bytes_accessed=6 << 20, transcendentals=0
        ),
    )(flat, gain, weights)


def score(masks, queries, one, two, rows_held):
    length, width = queries.shape
    lanes_n = GROUP * (width // HEADS)
    scores = []
    for g in range(HEADS // GROUP):
        cols = slice(g * lanes_n, (g + 1) * lanes_n)
        part = queries[:, cols]
        stacked = jnp.concatenate([part * masks[h : h + 1] for h in range(GROUP)], axis=0)
        keys = jnp.concatenate([rows_held[one, :, cols], rows_held[two, :, cols]], axis=0)
        scores.append(
            lax.dot_general(
                stacked, keys, (((1,), (1,)), ((), ())), preferred_element_type=jnp.float32
            )
        )
    return scores


def weigh(scores, width):
    to_log2 = (width // HEADS) ** -0.5 * math.log2(math.e)
    probs = []
    for part in scores:
        peak = jnp.max(part, axis=-1, keepdims=True)
        probs.append(jnp.exp2((part - peak) * to_log2).astype(jnp.bfloat16))
    return probs


def mix(ones, probs, one, two, rows_held, joined, row, length, width):
    head = width // HEADS
    lanes_n = GROUP * head
    lane = lax.broadcasted_iota(jnp.int32, (length, lanes_n), 1)
    for g in range(HEADS // GROUP):
        cols = slice(g * lanes_n, (g + 1) * lanes_n)
        vcols = slice(width + g * lanes_n, width + (g + 1) * lanes_n)
        values = jnp.concatenate([rows_held[one, :, vcols], rows_held[two, :, vcols]], axis=0)
        total = jnp.dot(probs[g], ones, preferred_element_type=jnp.float32)
        out = jnp.dot(probs[g], values, preferred_element_type=jnp.float32)
        denominator = jnp.where(lane < head, total[:length], total[length:])
        numerator = jnp.where(lane < head, out[:length], out[length:])
        joined[row : row + length, cols] = (numerator / denominator).astype(jnp.bfloat16)


def project_rows(blocks, w_held, rows_held, first, width):
    count = blocks.shape[0] // rows_held.shape[1]
    for at in (0, width):
        rows = jnp.dot(
            blocks, w_held[:, at : at + width], preferred_element_type=jnp.float32
        ).astype(jnp.bfloat16)
        rows_held[pl.ds(first, count), :, at : at + width] = rows.reshape(
            count, rows_held.shape[1], width
        )


class Spans:
    def __init__(self, meta_ref, slots, held, out_ref, out_sems):
        self.meta_ref, self.slots, self.held = meta_ref, slots, held
        self.out_ref, self.out_sems = out_ref, out_sems

    def span_at(self, position):
        return self.meta_ref[self.slots + position]

    def write(self, position):
        return pltpu.make_async_copy(
            self.held["out"].at[position],
            self.out_ref.at[self.span_at(position)],
            self.out_sems.at[position],
        )

    def step(self, group, live, load):
        held, meta_ref = self.held, self.meta_ref
        length, width = held["tokens"].shape[1:]
        head = width // HEADS
        lane = lax.broadcasted_iota(jnp.int32, (GROUP, GROUP * head), 1) // head
        which = lax.broadcasted_iota(jnp.int32, (GROUP, GROUP * head), 0)
        masks = (lane == which).astype(jnp.float32).astype(jnp.bfloat16)
        ones = jnp.ones((2 * length, 128), jnp.bfloat16)

        limit = held["rows"].shape[0] - 1
        spans = held["tokens"].shape[0]
        for t in range(0, 4, 2):
            positions = (group * 4 + t, group * 4 + t + 1)

            @pl.when(live(positions[0]) | live(positions[1]))
            def _():
                for position in positions:

                    @pl.when(live(position))
                    def _():
                        load(position)

                spots = [self.span_at(position) for position in positions]
                blocks = [
                    [jnp.minimum(meta_ref[n * spans + c], limit) for n in range(2)] for c in spots
                ]
                probs = [
                    weigh(score(masks, held["queries"][c], *pair, held["rows"]), width)
                    for c, pair in zip(spots, blocks)
                ]
                for i, pair in enumerate(blocks):
                    row = (t + i) * length
                    mix(ones, probs[i], *pair, held["rows"], held["joined"], row, length, width)

        projected = jnp.dot(
            held["joined"][...], held["w_out"][...], preferred_element_type=jnp.float32
        )
        for t in range(4):
            position = group * 4 + t

            @pl.when(live(position))
            def _():
                c = self.span_at(position)
                held["out"][position] = (
                    held["tokens"][c].astype(jnp.float32)
                    + projected[t * length : (t + 1) * length]
                ).astype(jnp.bfloat16)
                self.write(position).start()


def first_kernel(
    slots,
    meta_ref,
    tokens_ref,
    queries_ref,
    weights_ref,
    blocks_ref,
    rows_ref,
    out_ref,
    tokens_held,
    queries_held,
    w_held,
    w_out_held,
    blocks_held,
    rows_held,
    joined,
    out_held,
    in_sems,
    block_sems,
    row_sems,
    out_sems,
):
    spans, length, width = tokens_held.shape
    n_late = meta_ref[slots + spans]
    tile = 4
    tiles = blocks_held.shape[0] // tile
    loads = [
        pltpu.make_async_copy(
            weights_ref.at[:, pl.ds(width, 2 * width)], w_held, in_sems.at[0]
        ),
        pltpu.make_async_copy(
            weights_ref.at[:, pl.ds(3 * width, width)], w_out_held, in_sems.at[1]
        ),
        pltpu.make_async_copy(queries_ref, queries_held, in_sems.at[2]),
        pltpu.make_async_copy(tokens_ref, tokens_held, in_sems.at[3]),
    ]

    def block(i):
        at = pl.ds(pl.multiple_of(i * tile, tile), tile)
        return pltpu.make_async_copy(blocks_ref.at[at], blocks_held.at[at], block_sems.at[i])

    def row(i):
        at = pl.ds(pl.multiple_of(i * tile, tile), tile)
        return pltpu.make_async_copy(rows_held.at[at], rows_ref.at[at], row_sems.at[i])

    block(0).start()
    loads[0].start()
    for i in range(1, tiles):
        block(i).start()
    for load in loads[1:]:
        load.start()
    loads[0].wait()

    def keys(i, _):
        block(i).wait()
        first = pl.multiple_of(i * tile, tile)
        blocks = blocks_held[pl.ds(first, tile)].reshape(tile * length, width)
        project_rows(blocks, w_held, rows_held, first, width)
        row(i).start()
        return 0

    lax.fori_loop(0, tiles, keys, 0)
    for load in loads[1:]:
        load.wait()
    held = dict(
        tokens=tokens_held,
        queries=queries_held,
        rows=rows_held,
        joined=joined,
        w_out=w_out_held,
        out=out_held,
    )
    work = Spans(meta_ref, slots, held, out_ref, out_sems)

    def live(position):
        return position >= n_late

    for group in range(spans // 4):

        @pl.when(live(4 * group + 3))
        def _():
            work.step(group, live, lambda position: None)

    for position in range(spans):

        @pl.when(live(position))
        def _():
            work.write(position).wait()

    for i in range(tiles):
        row(i).wait()


def last_kernel(
    slots,
    holders,
    meta_ref,
    tokens_ref,
    queries_ref,
    weights_ref,
    rows_ref,
    second_ref,
    early_ref,
    out_ref,
    tokens_held,
    queries_held,
    w_held,
    blocks_held,
    rows_held,
    joined,
    out_held,
    in_sems,
    block_sems,
    span_sems,
    row_sems,
    out_sems,
):
    del early_ref
    spans, length, width = tokens_held.shape
    extra = blocks_held.shape[0]
    n_late = meta_ref[slots + spans]
    n_extra = meta_ref[slots + spans + 1]
    loads = [
        pltpu.make_async_copy(
            weights_ref.at[:, pl.ds((1 + i) * width, width)], w_held.at[i], in_sems.at[i]
        )
        for i in range(3)
    ]

    def block(i):
        return pltpu.make_async_copy(
            second_ref.at[meta_ref[slots + spans + 2 + i]], blocks_held.at[i], block_sems.at[i]
        )

    def span_loads(position):
        c = meta_ref[slots + position]
        return (
            pltpu.make_async_copy(
                queries_ref.at[c], queries_held.at[c], span_sems.at[0, position]
            ),
            pltpu.make_async_copy(
                tokens_ref.at[c], tokens_held.at[c], span_sems.at[1, position]
            ),
        )

    def early_rows(position, n):
        p = meta_ref[n * spans + meta_ref[slots + position]]
        copy = pltpu.make_async_copy(
            rows_ref.at[jnp.minimum(p, holders - 1)],
            rows_held.at[jnp.minimum(p, holders - 1)],
            row_sems.at[n, position],
        )
        return p < holders, copy

    for i in range(extra):

        @pl.when(i < n_extra)
        def _():
            block(i).start()

    for load in loads:
        load.start()

    def start(position, _):
        @pl.when(position < n_late)
        def _():
            for copy in span_loads(position):
                copy.start()
            for n in range(2):
                early, copy = early_rows(position, n)

                @pl.when(early)
                def _():
                    copy.start()

        return 0

    lax.fori_loop(0, spans, start, 0)
    for i in range(extra):

        @pl.when(i < n_extra)
        def _():
            block(i).wait()

    for n in range(2):
        loads[n].wait()
        for t in range(extra // 4):

            @pl.when(4 * t < n_extra)
            def _():
                blocks = blocks_held[4 * t : 4 * t + 4].reshape(4 * length, width)
                rows = jnp.dot(blocks, w_held[n], preferred_element_type=jnp.float32)
                rows_held[
                    holders + 4 * t : holders + 4 * t + 4, :, n * width : (n + 1) * width
                ] = rows.astype(jnp.bfloat16).reshape(4, length, width)

    loads[2].wait()
    held = dict(
        tokens=tokens_held,
        queries=queries_held,
        rows=rows_held,
        joined=joined,
        w_out=w_held.at[2],
        out=out_held,
    )
    work = Spans(meta_ref, slots, held, out_ref, out_sems)

    def live(position):
        return position < n_late

    def load(position):
        for copy in span_loads(position):
            copy.wait()
        for n in range(2):
            early, copy = early_rows(position, n)

            @pl.when(early)
            def _():
                copy.wait()

    for group in range(spans // 4):

        @pl.when(live(4 * group))
        def _():
            work.step(group, live, load)

    for position in range(spans):

        @pl.when(live(position))
        def _():
            work.write(position).wait()


def project_first(meta, tokens, queries, weights, first):
    spans, length, width = tokens.shape
    holders = first.shape[0]
    kind = tokens.dtype
    anywhere = pl.BlockSpec(memory_space=HBM)
    return pl.pallas_call(
        functools.partial(first_kernel, 2 * spans),
        out_shape=(
            jax.ShapeDtypeStruct((holders, length, 2 * width), kind),
            jax.ShapeDtypeStruct(tokens.shape, kind),
        ),
        grid_spec=pltpu.PrefetchScalarGridSpec(
            num_scalar_prefetch=1,
            grid=(1,),
            in_specs=[anywhere] * 4,
            out_specs=(anywhere, anywhere),
            scratch_shapes=[
                pltpu.VMEM(tokens.shape, kind),
                pltpu.VMEM(tokens.shape, kind),
                pltpu.VMEM((width, 2 * width), kind),
                pltpu.VMEM((width, width), kind),
                pltpu.VMEM(first.shape, kind),
                pltpu.VMEM((holders, length, 2 * width), kind),
                pltpu.VMEM((4 * length, width), kind),
                pltpu.VMEM(tokens.shape, kind),
                pltpu.SemaphoreType.DMA((4,)),
                pltpu.SemaphoreType.DMA((holders // 4,)),
                pltpu.SemaphoreType.DMA((holders // 4,)),
                pltpu.SemaphoreType.DMA((spans,)),
            ],
        ),
        compiler_params=pltpu.CompilerParams(vmem_limit_bytes=67_000_000),
        cost_estimate=pl.CostEstimate(
            flops=15 << 30, bytes_accessed=32 << 20, transcendentals=1 << 20
        ),
    )(meta, tokens, queries, weights, first)


def finish(meta, tokens, queries, weights, first_rows, second, early):
    spans, length, width = tokens.shape
    holders = first_rows.shape[0]
    extra = spans
    kind = tokens.dtype
    anywhere = pl.BlockSpec(memory_space=HBM)
    return pl.pallas_call(
        functools.partial(last_kernel, 2 * spans, holders),
        out_shape=jax.ShapeDtypeStruct(tokens.shape, kind),
        grid_spec=pltpu.PrefetchScalarGridSpec(
            num_scalar_prefetch=1,
            grid=(1,),
            in_specs=[anywhere] * 6,
            out_specs=anywhere,
            scratch_shapes=[
                pltpu.VMEM(tokens.shape, kind),
                pltpu.VMEM(tokens.shape, kind),
                pltpu.VMEM((3, width, width), kind),
                pltpu.VMEM((extra, length, width), kind),
                pltpu.VMEM((holders + extra, length, 2 * width), kind),
                pltpu.VMEM((4 * length, width), kind),
                pltpu.VMEM(tokens.shape, kind),
                pltpu.SemaphoreType.DMA((3,)),
                pltpu.SemaphoreType.DMA((extra,)),
                pltpu.SemaphoreType.DMA((2, spans)),
                pltpu.SemaphoreType.DMA((2, spans)),
                pltpu.SemaphoreType.DMA((spans,)),
            ],
        ),
        input_output_aliases={6: 0},
        compiler_params=pltpu.CompilerParams(vmem_limit_bytes=67_000_000),
        cost_estimate=pl.CostEstimate(
            flops=8 << 30, bytes_accessed=16 << 20, transcendentals=1 << 20
        ),
    )(meta, tokens, queries, weights, first_rows, second, early)


def shards(tokens, neighbours, database, norm_gain, q_weight, key_weight, value_weight, out_weight):
    spans, length, width = tokens.shape
    holders = lax.axis_size("db")
    slab = database.shape[0]
    wanted_ids = neighbours.T.reshape(-1)
    needed = wanted_ids.shape[0]
    extra = needed // 2
    holder_of = wanted_ids // slab
    local_row = wanted_ids % slab
    position = jnp.arange(needed, dtype=jnp.int32)
    turn = position % spans * 2 + position // spans
    earlier = turn[None, :] < turn[:, None]
    same = holder_of[None, :] == holder_of[:, None]
    rank_of = jnp.sum((same & earlier).astype(jnp.int32), axis=1)
    slot_of = rank_of * holders + holder_of
    hit = slot_of[:, None] == jnp.arange(2 * holders, dtype=jnp.int32)[None, :]
    wanted = jnp.sum(jnp.where(hit, local_row[:, None], 0), axis=0).reshape(2, holders)
    halves = jnp.stack(
        [
            jnp.concatenate([q_weight, key_weight], axis=1),
            jnp.concatenate([value_weight, out_weight], axis=1),
        ]
    )
    height, half = halves.shape[1:]
    ask = jnp.pad(
        wanted.T.astype(jnp.bfloat16)[:, None, :], ((0, 0), (0, height - 1), (0, 126))
    )
    parcels = jnp.concatenate([jnp.tile(halves, (holders // 2, 1, 1)), ask], axis=2)
    arrived = lax.all_to_all(parcels, "db", split_axis=0, concat_axis=0, tiled=True)
    incoming = arrived[:, 0, half : half + 2].T.astype(jnp.int32)
    rows = jnp.clip(incoming, 0, slab - 1)
    picked = gather_rows(database, rows[0])
    first = lax.all_to_all(picked, "db", split_axis=0, concat_axis=0, tiled=True)
    own = arrived[:, :, :half].reshape(holders * height, half)
    own, _ = lax.optimization_barrier((own, picked))
    size = lax.axis_size("dp")
    before = [(i, (i + 1) % size) for i in range(size)]
    after = [(i, (i + size - 1) % size) for i in range(size)]
    middle = own.shape[0] // 2
    left = lax.ppermute(own, "dp", before)
    right = lax.ppermute(own, "dp", after)
    late_rows, left, right = lax.optimization_barrier((rows[1], left, right))
    far_top = lax.ppermute(left[:middle], "dp", before)
    far_bottom = lax.ppermute(right[middle:], "dp", after)
    late, far_top, far_bottom = lax.optimization_barrier(
        (gather_rows(database, late_rows), far_top, far_bottom)
    )
    second = lax.all_to_all(late, "db", split_axis=0, concat_axis=0, tiled=True)
    mine = [own, left, right, far_top, far_bottom]
    swap = [(i, i ^ 1) for i in range(holders)]
    theirs = [lax.ppermute(piece, "db", swap) for piece in mine]
    where = jnp.stack([lax.axis_index("db") % 2, lax.axis_index("dp")]).astype(jnp.int32)
    weights = assemble(where, mine, theirs, size)

    extra_of = jnp.sum(jnp.where(earlier, rank_of[None, :], 0), axis=1)
    place = jnp.where(rank_of == 0, holder_of, holders + extra_of)
    chosen = (rank_of[:, None] == 1) & (
        extra_of[:, None] == jnp.arange(extra, dtype=jnp.int32)[None, :]
    )
    extras = jnp.sum(jnp.where(chosen, holder_of[:, None], 0), axis=0)
    span = jnp.arange(spans, dtype=jnp.int32)
    is_late = jnp.max(rank_of.reshape(2, spans), axis=0)
    n_late = jnp.sum(is_late)
    late_before = jnp.sum(jnp.where(span[None, :] < span[:, None], is_late[None, :], 0), axis=1)
    listed = jnp.where(is_late == 1, late_before, n_late + span - late_before)
    order = jnp.sum(jnp.where(listed[:, None] == span[None, :], span[:, None], 0), axis=0)
    meta = jnp.concatenate([place, order, n_late[None], jnp.sum(rank_of)[None], extras])

    queries = project_queries(
        tokens.reshape(-1, width), norm_gain.reshape(1, -1), weights
    ).reshape(tokens.shape)
    first_rows, early = project_first(meta, tokens, queries, weights, first)
    return finish(meta, tokens, queries, weights, first_rows, second, early)


def solution(mesh):
    both = P(("dp", "db"), None)
    placed = (
        P(("dp", "db"), None, None),
        both,
        P("db", None, None),
        P(),
        both,
        both,
        both,
        both,
    )
    return jax.shard_map(
        shards, mesh=mesh, in_specs=placed, out_specs=P(("dp", "db"), None, None), check_vma=False
    )
```

```python
import functools
import math

import jax
import jax.numpy as jnp
from jax import lax
from jax.experimental import pallas as pl
from jax.experimental.pallas import tpu as pltpu
from jax.sharding import PartitionSpec as P


HEADS = 16
GROUP = 2
ANY = pl.ANY
HBM = pltpu.MemorySpace.HBM


def gather_kernel(rows_ref, table_ref, out_ref, held, in_sems, out_sems):
    count = held.shape[0]

    def read(i):
        return pltpu.make_async_copy(table_ref.at[rows_ref[i]], held.at[i], in_sems.at[i])

    def write(i):
        return pltpu.make_async_copy(held.at[i], out_ref.at[i], out_sems.at[i])

    for i in range(count):
        read(i).start()
    for i in range(count):
        read(i).wait()
        write(i).start()
    for i in range(count):
        write(i).wait()


def gather_rows(table, rows):
    count = rows.shape[0]
    shape = (count,) + table.shape[1:]
    nbytes = 2 * count * table.shape[1] * table.shape[2]
    return pl.pallas_call(
        gather_kernel,
        out_shape=jax.ShapeDtypeStruct(shape, table.dtype),
        grid_spec=pltpu.PrefetchScalarGridSpec(
            num_scalar_prefetch=1,
            grid=(1,),
            in_specs=[pl.BlockSpec(memory_space=ANY)],
            out_specs=pl.BlockSpec(memory_space=ANY),
            scratch_shapes=[
                pltpu.VMEM(shape, table.dtype),
                pltpu.SemaphoreType.DMA((count,)),
                pltpu.SemaphoreType.DMA((count,)),
            ],
        ),
        cost_estimate=pl.CostEstimate(flops=0, bytes_accessed=2 * nbytes, transcendentals=0),
    )(rows, table)


def assemble_kernel(size, core_ref, *refs):
    n = (len(refs) - 4) // 2
    mine, theirs = refs[:n], refs[n : 2 * n]
    out_ref, held, in_sems, out_sems = refs[2 * n :]
    core, me = core_ref[0], core_ref[1]
    rows, half = mine[0].shape
    starts = [(me, 0), (lax.rem(me + size - 1, size), 0), (lax.rem(me + 1, size), 0)]
    starts += [(lax.rem(me + 2, size), 0), (lax.rem(me + 2, size), rows // 2)]
    copies = []
    for s, (side, source) in enumerate(((core, mine), (1 - core, theirs))):
        for i, ref in enumerate(source):
            piece, within = starts[i]
            height = ref.shape[0]
            at = pl.multiple_of(piece * rows + within, 16)
            left = pl.multiple_of(side * half, 128)
            spot = held.at[s, pl.ds(at, height)]
            read = pltpu.make_async_copy(ref, spot, in_sems.at[s * n + i])
            write = pltpu.make_async_copy(
                spot, out_ref.at[pl.ds(at, height), pl.ds(left, half)], out_sems.at[s * n + i]
            )
            copies.append((read, write))
    for read, _ in copies:
        read.start()
    for read, write in copies:
        read.wait()
        write.start()
    for _, write in copies:
        write.wait()


def assemble(where, mine, theirs, size):
    rows, half = mine[0].shape
    n = len(mine)
    return pl.pallas_call(
        functools.partial(assemble_kernel, size),
        out_shape=jax.ShapeDtypeStruct((size * rows, 2 * half), mine[0].dtype),
        grid_spec=pltpu.PrefetchScalarGridSpec(
            num_scalar_prefetch=1,
            grid=(1,),
            in_specs=[pl.BlockSpec(memory_space=ANY)] * (2 * n),
            out_specs=pl.BlockSpec(memory_space=ANY),
            scratch_shapes=[
                pltpu.VMEM((2, size * rows, half), mine[0].dtype),
                pltpu.SemaphoreType.DMA((2 * n,)),
                pltpu.SemaphoreType.DMA((2 * n,)),
            ],
        ),
        cost_estimate=pl.CostEstimate(flops=0, bytes_accessed=16 << 20, transcendentals=0),
    )(where, *mine, *theirs)


def query_kernel(tokens_ref, gain_ref, w_ref, out_ref):
    floated = tokens_ref[...].astype(jnp.float32)
    mean = jnp.mean(floated * floated, axis=-1, keepdims=True)
    normed = (floated * lax.rsqrt(mean + 1e-05) * gain_ref[...]).astype(jnp.bfloat16)
    out_ref[...] = jnp.dot(normed, w_ref[...], preferred_element_type=jnp.float32).astype(
        jnp.bfloat16
    )


def project_queries(flat, gain, weights, tile=256):
    rows, width = flat.shape
    return pl.pallas_call(
        query_kernel,
        out_shape=jax.ShapeDtypeStruct((rows, width), jnp.bfloat16),
        grid=(rows // tile,),
        in_specs=[
            pl.BlockSpec((tile, width), lambda i: (i, 0)),
            pl.BlockSpec((1, width), lambda i: (0, 0)),
            pl.BlockSpec((width, width), lambda i: (0, 0)),
        ],
        out_specs=pl.BlockSpec((tile, width), lambda i: (i, 0)),
        cost_estimate=pl.CostEstimate(
            flops=2 * rows * width * width, bytes_accessed=6 << 20, transcendentals=0
        ),
    )(flat, gain, weights)


def score(masks, queries, one, two, rows_held):
    length, width = queries.shape
    lanes_n = GROUP * (width // HEADS)
    scores = []
    for g in range(HEADS // GROUP):
        cols = slice(g * lanes_n, (g + 1) * lanes_n)
        part = queries[:, cols]
        stacked = jnp.concatenate([part * masks[h : h + 1] for h in range(GROUP)], axis=0)
        keys = jnp.concatenate([rows_held[one, :, cols], rows_held[two, :, cols]], axis=0)
        scores.append(
            lax.dot_general(
                stacked, keys, (((1,), (1,)), ((), ())), preferred_element_type=jnp.float32
            )
        )
    return scores


def weigh(scores, width):
    to_log2 = (width // HEADS) ** -0.5 * math.log2(math.e)
    weighed = []
    for part in scores:
        peak = jnp.max(part, axis=-1, keepdims=True)
        exponent = jnp.exp2((part - peak) * to_log2)
        total = jnp.sum(exponent, axis=-1, keepdims=True)
        weighed.append((exponent.astype(jnp.bfloat16), total))
    return weighed


def mix(weighed, one, two, rows_held, joined, row, length, width):
    head = width // HEADS
    lanes_n = GROUP * head
    lane = lax.broadcasted_iota(jnp.int32, (length, lanes_n), 1)
    for g in range(HEADS // GROUP):
        cols = slice(g * lanes_n, (g + 1) * lanes_n)
        vcols = slice(width + g * lanes_n, width + (g + 1) * lanes_n)
        values = jnp.concatenate([rows_held[one, :, vcols], rows_held[two, :, vcols]], axis=0)
        probs, total = weighed[g]
        total = jnp.broadcast_to(total, (2 * length, lanes_n))
        out = jnp.dot(probs, values, preferred_element_type=jnp.float32)
        denominator = jnp.where(lane < head, total[:length], total[length:])
        numerator = jnp.where(lane < head, out[:length], out[length:])
        joined[row : row + length, cols] = (numerator / denominator).astype(jnp.bfloat16)


def project_rows(blocks, w_held, rows_held, first, width):
    count = blocks.shape[0] // rows_held.shape[1]
    for at in (0, width):
        rows = jnp.dot(
            blocks, w_held[:, at : at + width], preferred_element_type=jnp.float32
        ).astype(jnp.bfloat16)
        rows_held[pl.ds(first, count), :, at : at + width] = rows.reshape(
            count, rows_held.shape[1], width
        )


class Spans:
    def __init__(self, meta_ref, slots, held, out_ref, out_sems):
        self.meta_ref, self.slots, self.held = meta_ref, slots, held
        self.out_ref, self.out_sems = out_ref, out_sems

    def span_at(self, position):
        return self.meta_ref[self.slots + position]

    def write(self, position):
        return pltpu.make_async_copy(
            self.held["out"].at[position],
            self.out_ref.at[self.span_at(position)],
            self.out_sems.at[position],
        )

    def step(self, group, live, load):
        held, meta_ref = self.held, self.meta_ref
        length, width = held["tokens"].shape[1:]
        head = width // HEADS
        lane = lax.broadcasted_iota(jnp.int32, (GROUP, GROUP * head), 1) // head
        which = lax.broadcasted_iota(jnp.int32, (GROUP, GROUP * head), 0)
        masks = (lane == which).astype(jnp.float32).astype(jnp.bfloat16)

        limit = held["rows"].shape[0] - 1
        spans = held["tokens"].shape[0]
        for t in range(0, 4, 2):
            positions = (group * 4 + t, group * 4 + t + 1)

            @pl.when(live(positions[0]) | live(positions[1]))
            def _():
                for position in positions:

                    @pl.when(live(position))
                    def _():
                        load(position)

                spots = [self.span_at(position) for position in positions]
                blocks = [
                    [jnp.minimum(meta_ref[n * spans + c], limit) for n in range(2)] for c in spots
                ]
                weighed = [
                    weigh(score(masks, held["queries"][c], *pair, held["rows"]), width)
                    for c, pair in zip(spots, blocks)
                ]
                for i, pair in enumerate(blocks):
                    row = (t + i) * length
                    mix(weighed[i], *pair, held["rows"], held["joined"], row, length, width)

        projected = jnp.dot(
            held["joined"][...], held["w_out"][...], preferred_element_type=jnp.float32
        )
        for t in range(4):
            position = group * 4 + t

            @pl.when(live(position))
            def _():
                c = self.span_at(position)
                held["out"][position] = (
                    held["tokens"][c].astype(jnp.float32)
                    + projected[t * length : (t + 1) * length]
                ).astype(jnp.bfloat16)
                self.write(position).start()


def first_kernel(
    slots,
    meta_ref,
    tokens_ref,
    queries_ref,
    weights_ref,
    blocks_ref,
    rows_ref,
    out_ref,
    tokens_held,
    queries_held,
    w_held,
    w_out_held,
    blocks_held,
    rows_held,
    joined,
    out_held,
    in_sems,
    block_sems,
    row_sems,
    out_sems,
):
    spans, length, width = tokens_held.shape
    n_late = meta_ref[slots + spans]
    tile = 4
    tiles = blocks_held.shape[0] // tile
    loads = [
        pltpu.make_async_copy(
            weights_ref.at[:, pl.ds(width, 2 * width)], w_held, in_sems.at[0]
        ),
        pltpu.make_async_copy(
            weights_ref.at[:, pl.ds(3 * width, width)], w_out_held, in_sems.at[1]
        ),
        pltpu.make_async_copy(queries_ref, queries_held, in_sems.at[2]),
        pltpu.make_async_copy(tokens_ref, tokens_held, in_sems.at[3]),
    ]

    def block(i):
        at = pl.ds(pl.multiple_of(i * tile, tile), tile)
        return pltpu.make_async_copy(blocks_ref.at[at], blocks_held.at[at], block_sems.at[i])

    def row(i):
        at = pl.ds(pl.multiple_of(i * tile, tile), tile)
        return pltpu.make_async_copy(rows_held.at[at], rows_ref.at[at], row_sems.at[i])

    block(0).start()
    loads[0].start()
    for i in range(1, tiles):
        block(i).start()
    for load in loads[1:]:
        load.start()
    loads[0].wait()

    def keys(i, _):
        block(i).wait()
        first = pl.multiple_of(i * tile, tile)
        blocks = blocks_held[pl.ds(first, tile)].reshape(tile * length, width)
        project_rows(blocks, w_held, rows_held, first, width)
        row(i).start()
        return 0

    lax.fori_loop(0, tiles, keys, 0)
    for load in loads[1:]:
        load.wait()
    held = dict(
        tokens=tokens_held,
        queries=queries_held,
        rows=rows_held,
        joined=joined,
        w_out=w_out_held,
        out=out_held,
    )
    work = Spans(meta_ref, slots, held, out_ref, out_sems)

    def live(position):
        return position >= n_late

    for group in range(spans // 4):

        @pl.when(live(4 * group + 3))
        def _():
            work.step(group, live, lambda position: None)

    for position in range(spans):

        @pl.when(live(position))
        def _():
            work.write(position).wait()

    for i in range(tiles):
        row(i).wait()


def last_kernel(
    slots,
    holders,
    meta_ref,
    tokens_ref,
    queries_ref,
    weights_ref,
    rows_ref,
    second_ref,
    early_ref,
    out_ref,
    tokens_held,
    queries_held,
    w_held,
    blocks_held,
    rows_held,
    joined,
    out_held,
    in_sems,
    block_sems,
    span_sems,
    row_sems,
    out_sems,
):
    del early_ref
    spans, length, width = tokens_held.shape
    extra = blocks_held.shape[0]
    n_late = meta_ref[slots + spans]
    n_extra = meta_ref[slots + spans + 1]
    loads = [
        pltpu.make_async_copy(
            weights_ref.at[:, pl.ds((1 + i) * width, width)], w_held.at[i], in_sems.at[i]
        )
        for i in range(3)
    ]

    def block(i):
        return pltpu.make_async_copy(
            second_ref.at[meta_ref[slots + spans + 2 + i]], blocks_held.at[i], block_sems.at[i]
        )

    def span_loads(position):
        c = meta_ref[slots + position]
        return (
            pltpu.make_async_copy(
                queries_ref.at[c], queries_held.at[c], span_sems.at[0, position]
            ),
            pltpu.make_async_copy(
                tokens_ref.at[c], tokens_held.at[c], span_sems.at[1, position]
            ),
        )

    def early_rows(position, n):
        p = meta_ref[n * spans + meta_ref[slots + position]]
        copy = pltpu.make_async_copy(
            rows_ref.at[jnp.minimum(p, holders - 1)],
            rows_held.at[jnp.minimum(p, holders - 1)],
            row_sems.at[n, position],
        )
        return p < holders, copy

    for i in range(extra):

        @pl.when(i < n_extra)
        def _():
            block(i).start()

    for load in loads:
        load.start()

    def start(position, _):
        @pl.when(position < n_late)
        def _():
            for copy in span_loads(position):
                copy.start()
            for n in range(2):
                early, copy = early_rows(position, n)

                @pl.when(early)
                def _():
                    copy.start()

        return 0

    lax.fori_loop(0, spans, start, 0)
    for i in range(extra):

        @pl.when(i < n_extra)
        def _():
            block(i).wait()

    for n in range(2):
        loads[n].wait()
        for t in range(extra // 4):

            @pl.when(4 * t < n_extra)
            def _():
                blocks = blocks_held[4 * t : 4 * t + 4].reshape(4 * length, width)
                rows = jnp.dot(blocks, w_held[n], preferred_element_type=jnp.float32)
                rows_held[
                    holders + 4 * t : holders + 4 * t + 4, :, n * width : (n + 1) * width
                ] = rows.astype(jnp.bfloat16).reshape(4, length, width)

    loads[2].wait()
    held = dict(
        tokens=tokens_held,
        queries=queries_held,
        rows=rows_held,
        joined=joined,
        w_out=w_held.at[2],
        out=out_held,
    )
    work = Spans(meta_ref, slots, held, out_ref, out_sems)

    def live(position):
        return position < n_late

    def load(position):
        for copy in span_loads(position):
            copy.wait()
        for n in range(2):
            early, copy = early_rows(position, n)

            @pl.when(early)
            def _():
                copy.wait()

    for group in range(spans // 4):

        @pl.when(live(4 * group))
        def _():
            work.step(group, live, load)

    for position in range(spans):

        @pl.when(live(position))
        def _():
            work.write(position).wait()


def project_first(meta, tokens, queries, weights, first):
    spans, length, width = tokens.shape
    holders = first.shape[0]
    kind = tokens.dtype
    anywhere = pl.BlockSpec(memory_space=HBM)
    return pl.pallas_call(
        functools.partial(first_kernel, 2 * spans),
        out_shape=(
            jax.ShapeDtypeStruct((holders, length, 2 * width), kind),
            jax.ShapeDtypeStruct(tokens.shape, kind),
        ),
        grid_spec=pltpu.PrefetchScalarGridSpec(
            num_scalar_prefetch=1,
            grid=(1,),
            in_specs=[anywhere] * 4,
            out_specs=(anywhere, anywhere),
            scratch_shapes=[
                pltpu.VMEM(tokens.shape, kind),
                pltpu.VMEM(tokens.shape, kind),
                pltpu.VMEM((width, 2 * width), kind),
                pltpu.VMEM((width, width), kind),
                pltpu.VMEM(first.shape, kind),
                pltpu.VMEM((holders, length, 2 * width), kind),
                pltpu.VMEM((4 * length, width), kind),
                pltpu.VMEM(tokens.shape, kind),
                pltpu.SemaphoreType.DMA((4,)),
                pltpu.SemaphoreType.DMA((holders // 4,)),
                pltpu.SemaphoreType.DMA((holders // 4,)),
                pltpu.SemaphoreType.DMA((spans,)),
            ],
        ),
        compiler_params=pltpu.CompilerParams(vmem_limit_bytes=67_000_000),
        cost_estimate=pl.CostEstimate(
            flops=15 << 30, bytes_accessed=32 << 20, transcendentals=1 << 20
        ),
    )(meta, tokens, queries, weights, first)


def finish(meta, tokens, queries, weights, first_rows, second, early):
    spans, length, width = tokens.shape
    holders = first_rows.shape[0]
    extra = spans
    kind = tokens.dtype
    anywhere = pl.BlockSpec(memory_space=HBM)
    return pl.pallas_call(
        functools.partial(last_kernel, 2 * spans, holders),
        out_shape=jax.ShapeDtypeStruct(tokens.shape, kind),
        grid_spec=pltpu.PrefetchScalarGridSpec(
            num_scalar_prefetch=1,
            grid=(1,),
            in_specs=[anywhere] * 6,
            out_specs=anywhere,
            scratch_shapes=[
                pltpu.VMEM(tokens.shape, kind),
                pltpu.VMEM(tokens.shape, kind),
                pltpu.VMEM((3, width, width), kind),
                pltpu.VMEM((extra, length, width), kind),
                pltpu.VMEM((holders + extra, length, 2 * width), kind),
                pltpu.VMEM((4 * length, width), kind),
                pltpu.VMEM(tokens.shape, kind),
                pltpu.SemaphoreType.DMA((3,)),
                pltpu.SemaphoreType.DMA((extra,)),
                pltpu.SemaphoreType.DMA((2, spans)),
                pltpu.SemaphoreType.DMA((2, spans)),
                pltpu.SemaphoreType.DMA((spans,)),
            ],
        ),
        input_output_aliases={6: 0},
        compiler_params=pltpu.CompilerParams(vmem_limit_bytes=67_000_000),
        cost_estimate=pl.CostEstimate(
            flops=8 << 30, bytes_accessed=16 << 20, transcendentals=1 << 20
        ),
    )(meta, tokens, queries, weights, first_rows, second, early)


def shards(tokens, neighbours, database, norm_gain, q_weight, key_weight, value_weight, out_weight):
    spans, length, width = tokens.shape
    holders = lax.axis_size("db")
    slab = database.shape[0]
    wanted_ids = neighbours.T.reshape(-1)
    needed = wanted_ids.shape[0]
    extra = needed // 2
    holder_of = wanted_ids // slab
    local_row = wanted_ids % slab
    position = jnp.arange(needed, dtype=jnp.int32)
    turn = position % spans * 2 + position // spans
    earlier = turn[None, :] < turn[:, None]
    same = holder_of[None, :] == holder_of[:, None]
    rank_of = jnp.sum((same & earlier).astype(jnp.int32), axis=1)
    slot_of = rank_of * holders + holder_of
    hit = slot_of[:, None] == jnp.arange(2 * holders, dtype=jnp.int32)[None, :]
    wanted = jnp.sum(jnp.where(hit, local_row[:, None], 0), axis=0).reshape(2, holders)
    halves = jnp.stack(
        [
            jnp.concatenate([q_weight, key_weight], axis=1),
            jnp.concatenate([value_weight, out_weight], axis=1),
        ]
    )
    height, half = halves.shape[1:]
    ask = jnp.pad(
        wanted.T.astype(jnp.bfloat16)[:, None, :], ((0, 0), (0, height - 1), (0, 126))
    )
    parcels = jnp.concatenate([jnp.tile(halves, (holders // 2, 1, 1)), ask], axis=2)
    arrived = lax.all_to_all(parcels, "db", split_axis=0, concat_axis=0, tiled=True)
    incoming = arrived[:, 0, half : half + 2].T.astype(jnp.int32)
    rows = jnp.clip(incoming, 0, slab - 1)
    picked = gather_rows(database, rows[0])
    first = lax.all_to_all(picked, "db", split_axis=0, concat_axis=0, tiled=True)
    own = arrived[:, :, :half].reshape(holders * height, half)
    own, _ = lax.optimization_barrier((own, picked))
    size = lax.axis_size("dp")
    before = [(i, (i + 1) % size) for i in range(size)]
    after = [(i, (i + size - 1) % size) for i in range(size)]
    middle = own.shape[0] // 2
    left = lax.ppermute(own, "dp", before)
    right = lax.ppermute(own, "dp", after)
    late_rows, left, right = lax.optimization_barrier((rows[1], left, right))
    far_top = lax.ppermute(left[:middle], "dp", before)
    far_bottom = lax.ppermute(right[middle:], "dp", after)
    late, far_top, far_bottom = lax.optimization_barrier(
        (gather_rows(database, late_rows), far_top, far_bottom)
    )
    second = lax.all_to_all(late, "db", split_axis=0, concat_axis=0, tiled=True)
    mine = [own, left, right, far_top, far_bottom]
    swap = [(i, i ^ 1) for i in range(holders)]
    theirs = [lax.ppermute(piece, "db", swap) for piece in mine]
    where = jnp.stack([lax.axis_index("db") % 2, lax.axis_index("dp")]).astype(jnp.int32)
    weights = assemble(where, mine, theirs, size)

    rank_of, _ = lax.optimization_barrier((rank_of, picked))
    extra_of = jnp.sum(jnp.where(earlier, rank_of[None, :], 0), axis=1)
    place = jnp.where(rank_of == 0, holder_of, holders + extra_of)
    chosen = (rank_of[:, None] == 1) & (
        extra_of[:, None] == jnp.arange(extra, dtype=jnp.int32)[None, :]
    )
    extras = jnp.sum(jnp.where(chosen, holder_of[:, None], 0), axis=0)
    span = jnp.arange(spans, dtype=jnp.int32)
    is_late = jnp.max(rank_of.reshape(2, spans), axis=0)
    n_late = jnp.sum(is_late)
    late_before = jnp.sum(jnp.where(span[None, :] < span[:, None], is_late[None, :], 0), axis=1)
    listed = jnp.where(is_late == 1, late_before, n_late + span - late_before)
    order = jnp.sum(jnp.where(listed[:, None] == span[None, :], span[:, None], 0), axis=0)
    meta = jnp.concatenate([place, order, n_late[None], jnp.sum(rank_of)[None], extras])

    queries = project_queries(
        tokens.reshape(-1, width), norm_gain.reshape(1, -1), weights
    ).reshape(tokens.shape)
    first_rows, early = project_first(meta, tokens, queries, weights, first)
    return finish(meta, tokens, queries, weights, first_rows, second, early)


def solution(mesh):
    both = P(("dp", "db"), None)
    placed = (
        P(("dp", "db"), None, None),
        both,
        P("db", None, None),
        P(),
        both,
        both,
        both,
        both,
    )
    return jax.shard_map(
        shards, mesh=mesh, in_specs=placed, out_specs=P(("dp", "db"), None, None), check_vma=False
    )
```

```python
import functools
import math

import jax
import jax.numpy as jnp
from jax import lax
from jax.experimental import pallas as pl
from jax.experimental.pallas import tpu as pltpu
from jax.sharding import PartitionSpec as P


HEADS = 16
GROUP = 2
ANY = pl.ANY
HBM = pltpu.MemorySpace.HBM


def gather_kernel(rows_ref, table_ref, out_ref, held, in_sems, out_sems):
    count = held.shape[0]

    def read(i):
        return pltpu.make_async_copy(table_ref.at[rows_ref[i]], held.at[i], in_sems.at[i])

    def write(i):
        return pltpu.make_async_copy(held.at[i], out_ref.at[i], out_sems.at[i])

    for i in range(count):
        read(i).start()
    for i in range(count):
        read(i).wait()
        write(i).start()
    for i in range(count):
        write(i).wait()


def gather_rows(table, rows):
    count = rows.shape[0]
    shape = (count,) + table.shape[1:]
    nbytes = 2 * count * table.shape[1] * table.shape[2]
    return pl.pallas_call(
        gather_kernel,
        out_shape=jax.ShapeDtypeStruct(shape, table.dtype),
        grid_spec=pltpu.PrefetchScalarGridSpec(
            num_scalar_prefetch=1,
            grid=(1,),
            in_specs=[pl.BlockSpec(memory_space=ANY)],
            out_specs=pl.BlockSpec(memory_space=ANY),
            scratch_shapes=[
                pltpu.VMEM(shape, table.dtype),
                pltpu.SemaphoreType.DMA((count,)),
                pltpu.SemaphoreType.DMA((count,)),
            ],
        ),
        cost_estimate=pl.CostEstimate(flops=0, bytes_accessed=2 * nbytes, transcendentals=0),
    )(rows, table)


def assemble_kernel(size, core_ref, *refs):
    n = (len(refs) - 4) // 2
    mine, theirs = refs[:n], refs[n : 2 * n]
    out_ref, held, in_sems, out_sems = refs[2 * n :]
    core, me = core_ref[0], core_ref[1]
    rows, half = mine[0].shape
    starts = [(me, 0), (lax.rem(me + size - 1, size), 0), (lax.rem(me + 1, size), 0)]
    starts += [(lax.rem(me + 2, size), 0), (lax.rem(me + 2, size), rows // 2)]
    copies = []
    for s, (side, source) in enumerate(((core, mine), (1 - core, theirs))):
        for i, ref in enumerate(source):
            piece, within = starts[i]
            height = ref.shape[0]
            at = pl.multiple_of(piece * rows + within, 16)
            left = pl.multiple_of(side * half, 128)
            spot = held.at[s, pl.ds(at, height)]
            read = pltpu.make_async_copy(ref, spot, in_sems.at[s * n + i])
            write = pltpu.make_async_copy(
                spot, out_ref.at[pl.ds(at, height), pl.ds(left, half)], out_sems.at[s * n + i]
            )
            copies.append((read, write))
    for read, _ in copies:
        read.start()
    for read, write in copies:
        read.wait()
        write.start()
    for _, write in copies:
        write.wait()


def assemble(where, mine, theirs, size):
    rows, half = mine[0].shape
    n = len(mine)
    return pl.pallas_call(
        functools.partial(assemble_kernel, size),
        out_shape=jax.ShapeDtypeStruct((size * rows, 2 * half), mine[0].dtype),
        grid_spec=pltpu.PrefetchScalarGridSpec(
            num_scalar_prefetch=1,
            grid=(1,),
            in_specs=[pl.BlockSpec(memory_space=ANY)] * (2 * n),
            out_specs=pl.BlockSpec(memory_space=ANY),
            scratch_shapes=[
                pltpu.VMEM((2, size * rows, half), mine[0].dtype),
                pltpu.SemaphoreType.DMA((2 * n,)),
                pltpu.SemaphoreType.DMA((2 * n,)),
            ],
        ),
        cost_estimate=pl.CostEstimate(flops=0, bytes_accessed=16 << 20, transcendentals=0),
    )(where, *mine, *theirs)


def query_kernel(tokens_ref, gain_ref, w_ref, out_ref):
    floated = tokens_ref[...].astype(jnp.float32)
    mean = jnp.mean(floated * floated, axis=-1, keepdims=True)
    normed = (floated * lax.rsqrt(mean + 1e-05) * gain_ref[...]).astype(jnp.bfloat16)
    out_ref[...] = jnp.dot(normed, w_ref[...], preferred_element_type=jnp.float32).astype(
        jnp.bfloat16
    )


def project_queries(flat, gain, weights, tile=256):
    rows, width = flat.shape
    return pl.pallas_call(
        query_kernel,
        out_shape=jax.ShapeDtypeStruct((rows, width), jnp.bfloat16),
        grid=(rows // tile,),
        in_specs=[
            pl.BlockSpec((tile, width), lambda i: (i, 0)),
            pl.BlockSpec((1, width), lambda i: (0, 0)),
            pl.BlockSpec((width, width), lambda i: (0, 0)),
        ],
        out_specs=pl.BlockSpec((tile, width), lambda i: (i, 0)),
        cost_estimate=pl.CostEstimate(
            flops=2 * rows * width * width, bytes_accessed=6 << 20, transcendentals=0
        ),
    )(flat, gain, weights)


def score(masks, queries, one, two, rows_held):
    length, width = queries.shape
    lanes_n = GROUP * (width // HEADS)
    scores = []
    for g in range(HEADS // GROUP):
        cols = slice(g * lanes_n, (g + 1) * lanes_n)
        part = queries[:, cols]
        stacked = jnp.concatenate([part * masks[h : h + 1] for h in range(GROUP)], axis=0)
        keys = jnp.concatenate([rows_held[one, :, cols], rows_held[two, :, cols]], axis=0)
        scores.append(
            lax.dot_general(
                stacked, keys, (((1,), (1,)), ((), ())), preferred_element_type=jnp.float32
            )
        )
    return scores


def weigh(scores, width):
    to_log2 = (width // HEADS) ** -0.5 * math.log2(math.e)
    probs = []
    for part in scores:
        peak = jnp.max(part, axis=-1, keepdims=True)
        probs.append(jnp.exp2((part - peak) * to_log2).astype(jnp.bfloat16))
    return probs


def mix(ones, probs, one, two, rows_held, joined, row, length, width):
    head = width // HEADS
    lanes_n = GROUP * head
    lane = lax.broadcasted_iota(jnp.int32, (length, lanes_n), 1)
    for g in range(HEADS // GROUP):
        cols = slice(g * lanes_n, (g + 1) * lanes_n)
        vcols = slice(width + g * lanes_n, width + (g + 1) * lanes_n)
        values = jnp.concatenate([rows_held[one, :, vcols], rows_held[two, :, vcols]], axis=0)
        total = jnp.dot(probs[g], ones, preferred_element_type=jnp.float32)
        out = jnp.dot(probs[g], values, preferred_element_type=jnp.float32)
        denominator = jnp.where(lane < head, total[:length], total[length:])
        numerator = jnp.where(lane < head, out[:length], out[length:])
        joined[row : row + length, cols] = (numerator / denominator).astype(jnp.bfloat16)


def project_rows(blocks, w_held, rows_held, first, width):
    count = blocks.shape[0] // rows_held.shape[1]
    for at in (0, width):
        rows = jnp.dot(
            blocks, w_held[:, at : at + width], preferred_element_type=jnp.float32
        ).astype(jnp.bfloat16)
        rows_held[pl.ds(first, count), :, at : at + width] = rows.reshape(
            count, rows_held.shape[1], width
        )


class Spans:
    def __init__(self, meta_ref, slots, held, out_ref, out_sems):
        self.meta_ref, self.slots, self.held = meta_ref, slots, held
        self.out_ref, self.out_sems = out_ref, out_sems

    def span_at(self, position):
        return self.meta_ref[self.slots + position]

    def write(self, position):
        return pltpu.make_async_copy(
            self.held["out"].at[position],
            self.out_ref.at[self.span_at(position)],
            self.out_sems.at[position],
        )

    def step(self, group, live, load):
        held, meta_ref = self.held, self.meta_ref
        length, width = held["tokens"].shape[1:]
        head = width // HEADS
        lane = lax.broadcasted_iota(jnp.int32, (GROUP, GROUP * head), 1) // head
        which = lax.broadcasted_iota(jnp.int32, (GROUP, GROUP * head), 0)
        masks = (lane == which).astype(jnp.float32).astype(jnp.bfloat16)
        ones = jnp.ones((2 * length, 128), jnp.bfloat16)

        limit = held["rows"].shape[0] - 1
        spans = held["tokens"].shape[0]
        for t in range(0, 4, 2):
            positions = (group * 4 + t, group * 4 + t + 1)

            @pl.when(live(positions[0]) | live(positions[1]))
            def _():
                for position in positions:

                    @pl.when(live(position))
                    def _():
                        load(position)

                spots = [self.span_at(position) for position in positions]
                blocks = [
                    [jnp.minimum(meta_ref[n * spans + c], limit) for n in range(2)] for c in spots
                ]
                probs = [
                    weigh(score(masks, held["queries"][c], *pair, held["rows"]), width)
                    for c, pair in zip(spots, blocks)
                ]
                for i, pair in enumerate(blocks):
                    row = (t + i) * length
                    mix(ones, probs[i], *pair, held["rows"], held["joined"], row, length, width)

        projected = jnp.dot(
            held["joined"][...], held["w_out"][...], preferred_element_type=jnp.float32
        )
        for t in range(4):
            position = group * 4 + t

            @pl.when(live(position))
            def _():
                c = self.span_at(position)
                held["out"][position] = (
                    held["tokens"][c].astype(jnp.float32)
                    + projected[t * length : (t + 1) * length]
                ).astype(jnp.bfloat16)
                self.write(position).start()


def first_kernel(
    slots,
    meta_ref,
    tokens_ref,
    queries_ref,
    weights_ref,
    blocks_ref,
    rows_ref,
    out_ref,
    tokens_held,
    queries_held,
    w_held,
    w_out_held,
    blocks_held,
    rows_held,
    joined,
    out_held,
    in_sems,
    block_sems,
    row_sems,
    out_sems,
):
    spans, length, width = tokens_held.shape
    n_late = meta_ref[slots + spans]
    tile = 4
    tiles = blocks_held.shape[0] // tile
    loads = [
        pltpu.make_async_copy(
            weights_ref.at[:, pl.ds(width, 2 * width)], w_held, in_sems.at[0]
        ),
        pltpu.make_async_copy(
            weights_ref.at[:, pl.ds(3 * width, width)], w_out_held, in_sems.at[1]
        ),
        pltpu.make_async_copy(queries_ref, queries_held, in_sems.at[2]),
        pltpu.make_async_copy(tokens_ref, tokens_held, in_sems.at[3]),
    ]

    def block(i):
        at = pl.ds(pl.multiple_of(i * tile, tile), tile)
        return pltpu.make_async_copy(blocks_ref.at[at], blocks_held.at[at], block_sems.at[i])

    def row(i):
        at = pl.ds(pl.multiple_of(i * tile, tile), tile)
        return pltpu.make_async_copy(rows_held.at[at], rows_ref.at[at], row_sems.at[i])

    block(0).start()
    loads[0].start()
    for i in range(1, tiles):
        block(i).start()
    for load in loads[1:]:
        load.start()
    loads[0].wait()

    def keys(i, _):
        block(i).wait()
        first = pl.multiple_of(i * tile, tile)
        blocks = blocks_held[pl.ds(first, tile)].reshape(tile * length, width)
        project_rows(blocks, w_held, rows_held, first, width)
        row(i).start()
        return 0

    lax.fori_loop(0, tiles, keys, 0)
    for load in loads[1:]:
        load.wait()
    held = dict(
        tokens=tokens_held,
        queries=queries_held,
        rows=rows_held,
        joined=joined,
        w_out=w_out_held,
        out=out_held,
    )
    work = Spans(meta_ref, slots, held, out_ref, out_sems)

    def live(position):
        return position >= n_late

    for group in range(spans // 4):

        @pl.when(live(4 * group + 3))
        def _():
            work.step(group, live, lambda position: None)

    for position in range(spans):

        @pl.when(live(position))
        def _():
            work.write(position).wait()

    for i in range(tiles):
        row(i).wait()


def last_kernel(
    slots,
    holders,
    meta_ref,
    tokens_ref,
    queries_ref,
    weights_ref,
    rows_ref,
    second_ref,
    early_ref,
    out_ref,
    tokens_held,
    queries_held,
    w_held,
    blocks_held,
    rows_held,
    joined,
    out_held,
    in_sems,
    block_sems,
    span_sems,
    row_sems,
    out_sems,
):
    del early_ref
    spans, length, width = tokens_held.shape
    extra = blocks_held.shape[0]
    n_late = meta_ref[slots + spans]
    n_extra = meta_ref[slots + spans + 1]
    loads = [
        pltpu.make_async_copy(
            weights_ref.at[:, pl.ds((1 + i) * width, width)], w_held.at[i], in_sems.at[i]
        )
        for i in range(3)
    ]

    def block(i):
        return pltpu.make_async_copy(
            second_ref.at[meta_ref[slots + spans + 2 + i]], blocks_held.at[i], block_sems.at[i]
        )

    def span_loads(position):
        c = meta_ref[slots + position]
        return (
            pltpu.make_async_copy(
                queries_ref.at[c], queries_held.at[c], span_sems.at[0, position]
            ),
            pltpu.make_async_copy(
                tokens_ref.at[c], tokens_held.at[c], span_sems.at[1, position]
            ),
        )

    def early_rows(position, n):
        p = meta_ref[n * spans + meta_ref[slots + position]]
        copy = pltpu.make_async_copy(
            rows_ref.at[jnp.minimum(p, holders - 1)],
            rows_held.at[jnp.minimum(p, holders - 1)],
            row_sems.at[n, position],
        )
        return p < holders, copy

    for i in range(extra):

        @pl.when(i < n_extra)
        def _():
            block(i).start()

    for load in loads:
        load.start()

    def start(position, _):
        @pl.when(position < n_late)
        def _():
            for copy in span_loads(position):
                copy.start()
            for n in range(2):
                early, copy = early_rows(position, n)

                @pl.when(early)
                def _():
                    copy.start()

        return 0

    lax.fori_loop(0, spans, start, 0)
    for i in range(extra):

        @pl.when(i < n_extra)
        def _():
            block(i).wait()

    for n in range(2):
        loads[n].wait()
        for t in range(extra // 4):

            @pl.when(4 * t < n_extra)
            def _():
                blocks = blocks_held[4 * t : 4 * t + 4].reshape(4 * length, width)
                rows = jnp.dot(blocks, w_held[n], preferred_element_type=jnp.float32)
                rows_held[
                    holders + 4 * t : holders + 4 * t + 4, :, n * width : (n + 1) * width
                ] = rows.astype(jnp.bfloat16).reshape(4, length, width)

    loads[2].wait()
    held = dict(
        tokens=tokens_held,
        queries=queries_held,
        rows=rows_held,
        joined=joined,
        w_out=w_held.at[2],
        out=out_held,
    )
    work = Spans(meta_ref, slots, held, out_ref, out_sems)

    def live(position):
        return position < n_late

    def load(position):
        for copy in span_loads(position):
            copy.wait()
        for n in range(2):
            early, copy = early_rows(position, n)

            @pl.when(early)
            def _():
                copy.wait()

    for group in range(spans // 4):

        @pl.when(live(4 * group))
        def _():
            work.step(group, live, load)

    for position in range(spans):

        @pl.when(live(position))
        def _():
            work.write(position).wait()


def project_first(meta, tokens, queries, weights, first):
    spans, length, width = tokens.shape
    holders = first.shape[0]
    kind = tokens.dtype
    anywhere = pl.BlockSpec(memory_space=HBM)
    return pl.pallas_call(
        functools.partial(first_kernel, 2 * spans),
        out_shape=(
            jax.ShapeDtypeStruct((holders, length, 2 * width), kind),
            jax.ShapeDtypeStruct(tokens.shape, kind),
        ),
        grid_spec=pltpu.PrefetchScalarGridSpec(
            num_scalar_prefetch=1,
            grid=(1,),
            in_specs=[anywhere] * 4,
            out_specs=(anywhere, anywhere),
            scratch_shapes=[
                pltpu.VMEM(tokens.shape, kind),
                pltpu.VMEM(tokens.shape, kind),
                pltpu.VMEM((width, 2 * width), kind),
                pltpu.VMEM((width, width), kind),
                pltpu.VMEM(first.shape, kind),
                pltpu.VMEM((holders, length, 2 * width), kind),
                pltpu.VMEM((4 * length, width), kind),
                pltpu.VMEM(tokens.shape, kind),
                pltpu.SemaphoreType.DMA((4,)),
                pltpu.SemaphoreType.DMA((holders // 4,)),
                pltpu.SemaphoreType.DMA((holders // 4,)),
                pltpu.SemaphoreType.DMA((spans,)),
            ],
        ),
        compiler_params=pltpu.CompilerParams(vmem_limit_bytes=67_000_000),
        cost_estimate=pl.CostEstimate(
            flops=15 << 30, bytes_accessed=32 << 20, transcendentals=1 << 20
        ),
    )(meta, tokens, queries, weights, first)


def finish(meta, tokens, queries, weights, first_rows, second, early):
    spans, length, width = tokens.shape
    holders = first_rows.shape[0]
    extra = spans
    kind = tokens.dtype
    anywhere = pl.BlockSpec(memory_space=HBM)
    return pl.pallas_call(
        functools.partial(last_kernel, 2 * spans, holders),
        out_shape=jax.ShapeDtypeStruct(tokens.shape, kind),
        grid_spec=pltpu.PrefetchScalarGridSpec(
            num_scalar_prefetch=1,
            grid=(1,),
            in_specs=[anywhere] * 6,
            out_specs=anywhere,
            scratch_shapes=[
                pltpu.VMEM(tokens.shape, kind),
                pltpu.VMEM(tokens.shape, kind),
                pltpu.VMEM((3, width, width), kind),
                pltpu.VMEM((extra, length, width), kind),
                pltpu.VMEM((holders + extra, length, 2 * width), kind),
                pltpu.VMEM((4 * length, width), kind),
                pltpu.VMEM(tokens.shape, kind),
                pltpu.SemaphoreType.DMA((3,)),
                pltpu.SemaphoreType.DMA((extra,)),
                pltpu.SemaphoreType.DMA((2, spans)),
                pltpu.SemaphoreType.DMA((2, spans)),
                pltpu.SemaphoreType.DMA((spans,)),
            ],
        ),
        input_output_aliases={6: 0},
        compiler_params=pltpu.CompilerParams(vmem_limit_bytes=67_000_000),
        cost_estimate=pl.CostEstimate(
            flops=8 << 30, bytes_accessed=16 << 20, transcendentals=1 << 20
        ),
    )(meta, tokens, queries, weights, first_rows, second, early)


def shards(tokens, neighbours, database, norm_gain, q_weight, key_weight, value_weight, out_weight):
    spans, length, width = tokens.shape
    holders = lax.axis_size("db")
    slab = database.shape[0]
    wanted_ids = neighbours.T.reshape(-1)
    needed = wanted_ids.shape[0]
    extra = needed // 2
    holder_of = wanted_ids // slab
    local_row = wanted_ids % slab
    position = jnp.arange(needed, dtype=jnp.int32)
    turn = position % spans * 2 + position // spans
    earlier = turn[None, :] < turn[:, None]
    same = holder_of[None, :] == holder_of[:, None]
    rank_of = jnp.sum((same & earlier).astype(jnp.int32), axis=1)
    slot_of = rank_of * holders + holder_of
    hit = slot_of[:, None] == jnp.arange(2 * holders, dtype=jnp.int32)[None, :]
    wanted = jnp.sum(jnp.where(hit, local_row[:, None], 0), axis=0).reshape(2, holders)
    halves = jnp.stack(
        [
            jnp.concatenate([q_weight, key_weight], axis=1),
            jnp.concatenate([value_weight, out_weight], axis=1),
        ]
    )
    height, half = halves.shape[1:]
    ask = jnp.pad(
        wanted.T.astype(jnp.bfloat16)[:, None, :], ((0, 0), (0, height - 1), (0, 126))
    )
    parcels = jnp.concatenate([jnp.tile(halves, (holders // 2, 1, 1)), ask], axis=2)
    arrived = lax.all_to_all(parcels, "db", split_axis=0, concat_axis=0, tiled=True)
    incoming = arrived[:, 0, half : half + 2].T.astype(jnp.int32)
    rows = jnp.clip(incoming, 0, slab - 1)
    picked = gather_rows(database, rows[0])
    first = lax.all_to_all(picked, "db", split_axis=0, concat_axis=0, tiled=True)
    own = arrived[:, :, :half].reshape(holders * height, half)
    own, _ = lax.optimization_barrier((own, picked))
    size = lax.axis_size("dp")
    before = [(i, (i + 1) % size) for i in range(size)]
    after = [(i, (i + size - 1) % size) for i in range(size)]
    middle = own.shape[0] // 2
    left = lax.ppermute(own, "dp", before)
    right = lax.ppermute(own, "dp", after)
    late_rows, left, right = lax.optimization_barrier((rows[1], left, right))
    far_top = lax.ppermute(left[:middle], "dp", before)
    far_bottom = lax.ppermute(right[middle:], "dp", after)
    late, far_top, far_bottom = lax.optimization_barrier(
        (gather_rows(database, late_rows), far_top, far_bottom)
    )
    second = lax.all_to_all(late, "db", split_axis=0, concat_axis=0, tiled=True)
    mine = [own, left, right, far_top, far_bottom]
    swap = [(i, i ^ 1) for i in range(holders)]
    theirs = [lax.ppermute(piece, "db", swap) for piece in mine]
    where = jnp.stack([lax.axis_index("db") % 2, lax.axis_index("dp")]).astype(jnp.int32)
    weights = assemble(where, mine, theirs, size)

    rank_of, _ = lax.optimization_barrier((rank_of, picked))
    extra_of = jnp.sum(jnp.where(earlier, rank_of[None, :], 0), axis=1)
    place = jnp.where(rank_of == 0, holder_of, holders + extra_of)
    chosen = (rank_of[:, None] == 1) & (
        extra_of[:, None] == jnp.arange(extra, dtype=jnp.int32)[None, :]
    )
    extras = jnp.sum(jnp.where(chosen, holder_of[:, None], 0), axis=0)
    span = jnp.arange(spans, dtype=jnp.int32)
    is_late = jnp.max(rank_of.reshape(2, spans), axis=0)
    n_late = jnp.sum(is_late)
    late_before = jnp.sum(jnp.where(span[None, :] < span[:, None], is_late[None, :], 0), axis=1)
    listed = jnp.where(is_late == 1, late_before, n_late + span - late_before)
    order = jnp.sum(jnp.where(listed[:, None] == span[None, :], span[:, None], 0), axis=0)
    meta = jnp.concatenate([place, order, n_late[None], jnp.sum(rank_of)[None], extras])

    queries = project_queries(
        tokens.reshape(-1, width), norm_gain.reshape(1, -1), weights
    ).reshape(tokens.shape)
    first_rows, early = project_first(meta, tokens, queries, weights, first)
    return finish(meta, tokens, queries, weights, first_rows, second, early)


def solution(mesh):
    both = P(("dp", "db"), None)
    placed = (
        P(("dp", "db"), None, None),
        both,
        P("db", None, None),
        P(),
        both,
        both,
        both,
        both,
    )
    return jax.shard_map(
        shards, mesh=mesh, in_specs=placed, out_specs=P(("dp", "db"), None, None), check_vma=False
    )
```
